32 devices in a mesh: row: 4 (over z), mix: 8 (over y, x, core).
Axes of the slice: x: 2, y: 2, z: 4, core: 2. Of those that a mesh axis runs over, the one named last changes fastest.
Arguments:
- velocity: bfloat16 [64, 3, 8, 32, 128], P(None, None, 'mix', 'row'), may hold values from -6 to 6
- field_b: bfloat16 [64, 3, 8, 32, 128], P(None, None, 'mix', 'row'), may hold values from -6 to 6
- test_signs: int32 [384, 256], replicated, may hold values from 0 to 1
- row_signs: int32 [8, 32, 128], P('mix', 'row'), may hold values from 0 to 1
- sample_index: int32 [8, 4, 256], P('mix', 'row'), may hold values from 0 to 1023
Outputs:
- basis_rows: float32 [8, 4, 256, 256], P('mix', 'row')
- factor: float32 [256, 256], replicated
The draws below stay inside these ranges and needn't reach their ends.
Inputs may be any that keep to these rules, and one draw needn't show every extreme that they name: test_signs entries are bits; the test matrix is 2 test_signs - 1. row_signs entries are bits; the sign is 2 row_signs - 1. `sample_index`: a point of the device's own block, p = x_local 128 + y; repeats may occur.
All inputs are finite; a program needn't handle non-finite values.
Results may differ from the reference program's by a relative error of at most 0.0021.
Values may be sent and summed in bfloat16 or wider, within the bound.
No kernel may reach another device: no remote copies, remote signals or barrier semaphores. Data moves between devices by JAX's collectives and lax.ppermute only.
A program may use at most 64 MiB of HBM per device.

```python
import math
import jax
import jax.numpy as jnp
from jax import lax

SNAPS = 64
SKETCH = 256
CX = 8
CY = 128
SAMP = 256
NZ = 8
XB = 4
NX = 32


def touch_ends(values, key, low, high):
    dims = values.shape
    place = [jax.random.randint(jax.random.fold_in(key, axis), (), 0, dims[axis]) for axis in range(len(dims))]
    values = values.at[tuple(place)].set(low)
    longest = dims.index(max(dims))
    place[longest] = (place[longest] + 1) % dims[longest]
    return values.at[tuple(place)].set(high)


def block_levels(own_key, shape, pieces, low, top_value):
    def one(dim, blocks):
        steps = jax.random.uniform(jax.random.fold_in(jax.random.fold_in(own_key, 6), dim), (blocks,), jnp.float32, low / len(pieces), top_value / len(pieces))
        return jnp.repeat(jnp.exp(steps), shape[dim] // blocks).reshape((-1,) + (1,) * (len(shape) - dim - 1))

    factor_of = one(*pieces[0])
    for cut in pieces[1:]:
        factor_of = factor_of * one(*cut)
    return factor_of


def gaussian(rng, shape, deviation, most, shards=(), held_as=jnp.bfloat16):
    array = deviation * jax.random.normal(rng, shape, jnp.float32)
    if shards:
        array = array * block_levels(rng, shape, shards, -0.22, 0.18)
    return jnp.clip(array, -most, most).astype(held_as)


def setup_inputs(seed: int = 0) -> dict:
    seeds = jax.random.split(jax.random.key(seed), 6)
    return {
        "velocity": gaussian(seeds[0], (SNAPS, 3, NZ, NX, CY), 1.0, 6.0, ((2, 8), (3, 4))),
        "field_b": gaussian(seeds[1], (SNAPS, 3, NZ, NX, CY), 1.0, 6.0, ((2, 8), (3, 4))),
        "test_signs": touch_ends(jax.random.randint(seeds[2], (6 * SNAPS, SKETCH), 0, 2), jax.random.fold_in(seeds[2], 1), 0, 1).astype(jnp.int32),
        "row_signs": touch_ends(jax.random.randint(seeds[3], (NZ, NX, CY), 0, 2), jax.random.fold_in(seeds[3], 1), 0, 1).astype(jnp.int32),
        "sample_index": touch_ends(jax.random.randint(seeds[4], (NZ, XB, SAMP), 0, CX * CY), jax.random.fold_in(seeds[4], 1), 0, (CX * CY) - 1).astype(jnp.int32),
    }


def curl_plane(stencil_slab):
    center = stencil_slab[:, :, 1]

    def along_x(component):
        return (center[:, component, 2:, 1:-1] - center[:, component, :-2, 1:-1]) * 0.5

    def along_y(component):
        return (center[:, component, 1:-1, 2:] - center[:, component, 1:-1, :-2]) * 0.5

    def along_z(component):
        return (stencil_slab[:, component, 2, 1:-1, 1:-1] - stencil_slab[:, component, 0, 1:-1, 1:-1]) * 0.5
    current_x = along_y(2) - along_z(1)
    current_y = along_z(0) - along_x(2)
    current_z = along_x(1) - along_y(0)
    return jnp.stack([current_x, current_y, current_z], axis=1).astype(jnp.bfloat16)

def hadamard_table(planes):
    index_a = jnp.arange(planes, dtype=jnp.int32)[:, None]
    index_b = jnp.arange(planes, dtype=jnp.int32)[None, :]
    parity = jnp.zeros((planes, planes), jnp.int32)
    for level in range(max(planes.bit_length() - 1, 0)):
        parity = parity + index_a // (1 << level) % 2 * (index_b // (1 << level) % 2)
    return jnp.where(parity % 2 == 0, 1.0, -1.0).astype(jnp.float32)

def reference(velocity, field_b, test_signs, row_signs, sample_index):
    planes = field_b.shape[2]
    snaps = field_b.shape[0]
    sketch_width = test_signs.shape[1]
    padded = jnp.pad(field_b, ((0, 0), (0, 0), (1, 1), (1, 1), (1, 1)))
    test_matrix = (2 * test_signs - 1).astype(jnp.bfloat16)
    col_scale = 1.0 / math.sqrt(6 * snaps)

    def plane_sketch(plane):
        stencil_slab = lax.dynamic_slice_in_dim(padded, plane, 3, 2).astype(jnp.float32)
        current = curl_plane(stencil_slab)
        speed = lax.dynamic_index_in_dim(velocity, plane, 2, keepdims=False)
        snapshot = jnp.concatenate([speed, current], axis=1).reshape(6 * snaps, -1)
        sketch = lax.dot_general(snapshot.astype(jnp.float32), test_matrix.astype(jnp.float32), (((0,), (0,)), ((), ())), preferred_element_type=jnp.float32) * col_scale
        plane_signs = (2 * lax.dynamic_index_in_dim(row_signs, plane, 0, keepdims=False) - 1).astype(jnp.float32).reshape(-1)
        return sketch * plane_signs[:, None]
    signed = lax.map(plane_sketch, jnp.arange(planes, dtype=jnp.int32))
    hadamard = hadamard_table(planes)
    offsets = (jnp.arange(XB, dtype=jnp.int32) * (CX * CY)).astype(jnp.int32)
    flat_rows = (sample_index + offsets[None, :, None]).reshape(planes, -1).astype(jnp.int32)

    def mix_plane(target):
        gathered = jnp.take(signed, flat_rows[target], axis=1)
        weights = hadamard[target]
        return jnp.einsum('e,erk->rk', weights, gathered, precision=lax.Precision.HIGHEST) / math.sqrt(planes)
    picked = lax.map(mix_plane, jnp.arange(planes, dtype=jnp.int32))
    all_picked = picked.reshape(-1, sketch_width)
    gram_matrix = jnp.dot(all_picked.T.astype(jnp.float32), all_picked.astype(jnp.float32), precision=lax.Precision.HIGHEST, preferred_element_type=jnp.float32) / all_picked.shape[0]
    cholesky_low = jnp.linalg.cholesky(gram_matrix)
    factor = cholesky_low.T
    solved = jax.scipy.linalg.solve_triangular(cholesky_low, all_picked.T, lower=True)
    basis_rows = solved.T.reshape(sample_index.shape + (sketch_width,))
    return (basis_rows, factor)
```

```python
import math

import jax
import jax.numpy as jnp
from jax import lax
from jax.sharding import PartitionSpec as P

MESH_AXES = ("row", "mix")


def xor_route(count, bits):
    return [(i, i ^ bits) for i in range(count) if i ^ bits < count]


def turn_route(count, steps):
    return [(i, (i + steps) % count) for i in range(count)]


def neighbours(first, last, axis):
    size = lax.axis_size(axis)
    up = [(i, i + 1) for i in range(size - 1)]
    down = [(i + 1, i) for i in range(size - 1)]
    return lax.ppermute(last, axis, up), lax.ppermute(first, axis, down)


def curl(field_b):
    plane = field_b[:, :, 0]
    below, above = neighbours(plane[:, :2], plane[:, :2], "mix")
    left, right = neighbours(plane[:, 1:, :1], plane[:, 1:, -1:], "row")
    with_rims = jnp.concatenate([left, plane[:, 1:], right], axis=2).astype(jnp.float32)
    center = plane.astype(jnp.float32)
    over_z = (above.astype(jnp.float32) - below.astype(jnp.float32)) * 0.5
    over_x = (with_rims[:, :, 2:] - with_rims[:, :, :-2]) * 0.5
    wide = jnp.pad(center, ((0, 0), (0, 0), (0, 0), (1, 1)))
    over_y = (wide[..., 2:] - wide[..., :-2]) * 0.5
    current_x = over_y[:, 2] - over_z[:, 1]
    current_y = over_z[:, 0] - over_x[:, 1]
    current_z = over_x[:, 0] - over_y[:, 0]
    return jnp.stack([current_x, current_y, current_z], axis=1).astype(jnp.bfloat16)


def parity_sign(a, b):
    both = jnp.bitwise_and(a, b)
    return 1.0 - 2.0 * (lax.population_count(both) % 2).astype(jnp.float32)


def sampled_mixing(velocity, current, test_matrix, signs, sample_index):
    planes = lax.axis_size("mix")
    mine = lax.axis_index("mix")
    core = mine % 2
    hops = range(2, planes, 2)
    wanted = [sample_index] + [lax.ppermute(sample_index, "mix", xor_route(planes, k)) for k in hops]
    wanted = jnp.stack(wanted)
    snaps = velocity.shape[0]
    points = signs.shape[0]

    def flat(part):
        return part.reshape(3 * snaps, points) * signs

    by_part = test_matrix.reshape(snaps, 6, -1)
    for_velocity = by_part[:, :3].reshape(3 * snaps, -1)
    for_current = by_part[:, 3:].reshape(3 * snaps, -1)
    own_sign = (1 - 2 * core).astype(jnp.bfloat16)
    chosen = (wanted[:, None, :] == jnp.arange(points, dtype=jnp.int32)[None, :, None]).astype(jnp.bfloat16)

    def part_sum(part, matrix):
        own = flat(part)
        other = lax.ppermute(own, "mix", xor_route(planes, 1))
        both = jnp.concatenate([own, other])
        gathered = jnp.einsum("sp,tpk->tsk", both, chosen, preferred_element_type=jnp.float32).astype(jnp.bfloat16)
        twice = jnp.concatenate([own_sign * matrix, matrix])
        return jnp.einsum("sj,tsk->tjk", twice, gathered, preferred_element_type=jnp.float32)

    parts = part_sum(velocity, for_velocity) + part_sum(current, for_current)
    total = parity_sign(mine, mine - core) * parts[0]
    for slot, k in enumerate(hops):
        arrived = lax.ppermute(parts[slot + 1], "mix", xor_route(planes, k))
        total = total + parity_sign(mine, (mine ^ k) - core) * arrived
    return total * (1.0 / math.sqrt(6 * snaps) / math.sqrt(planes))


def whole_mixing(velocity, current, test_matrix, signs, sample_index):
    planes = lax.axis_size("mix")
    mine = lax.axis_index("mix")
    snaps = velocity.shape[0]
    snapshot = jnp.concatenate([velocity, current], axis=1).reshape(6 * snaps, -1) * signs
    values = lax.dot_general(
        snapshot, test_matrix, (((0,), (0,)), ((), ())), preferred_element_type=jnp.float32
    ) * (1.0 / math.sqrt(6 * snaps))
    for level in range(planes.bit_length() - 1):
        partner = lax.ppermute(values, "mix", xor_route(planes, 1 << level))
        upper_bit = mine // (1 << level) % 2
        values = jnp.where(upper_bit == 1, partner - values, values + partner)
    return jnp.take(values / math.sqrt(planes), sample_index, axis=0).T


def sum_over_mesh(gram):
    planes, blocks = lax.axis_size("mix"), lax.axis_size("row")
    if planes > 8 or blocks > 4:
        return lax.psum(gram, MESH_AXES)
    n = gram.shape[0]
    core = lax.axis_index("mix") % 2
    low, high = gram[: n // 2], gram[n // 2 :]
    half = jnp.where(core == 0, low, high)
    half = half + lax.ppermute(jnp.where(core == 0, high, low), "mix", xor_route(planes, 1))
    half = half + sum(lax.ppermute(half, "mix", xor_route(planes, k)) for k in range(2, planes, 2))
    half = half + sum(lax.ppermute(half, "row", turn_route(blocks, k)) for k in range(1, blocks))
    other = lax.ppermute(half, "mix", xor_route(planes, 1))
    return jnp.concatenate([jnp.where(core == 0, half, other), jnp.where(core == 0, other, half)])


def on_device(velocity, field_b, test_signs, row_signs, sample_index):
    snaps = field_b.shape[0]
    sketch_width = test_signs.shape[1]
    planes, blocks = lax.axis_size("mix"), lax.axis_size("row")
    samples = sample_index.shape[-1]
    points = row_signs.size
    test_matrix = (2 * test_signs - 1).astype(jnp.bfloat16)
    signs = (2 * row_signs - 1).astype(jnp.bfloat16).reshape(-1)
    current = curl(field_b)
    sampled_bytes = (planes // 2 - 1) * samples * sketch_width
    whole_bytes = (planes.bit_length() - 1) * points * sketch_width
    mixing = sampled_mixing if sampled_bytes < whole_bytes else whole_mixing
    picked = mixing(velocity[:, :, 0], current, test_matrix, signs, sample_index.reshape(-1))
    gram = jnp.einsum(
        "ik,jk->ij", picked, picked, precision=lax.Precision.HIGHEST, preferred_element_type=jnp.float32
    ) * (1.0 / (planes * blocks * samples))
    lower = jnp.linalg.cholesky(sum_over_mesh(gram))
    solved = jax.scipy.linalg.solve_triangular(lower, picked, lower=True)
    return solved.T.reshape(sample_index.shape + (sketch_width,)), lower.T


def solution(mesh):
    return jax.shard_map(
        on_device,
        mesh=mesh,
        in_specs=(
            P(None, None, "mix", "row", None),
            P(None, None, "mix", "row", None),
            P(),
            P("mix", "row", None),
            P("mix", "row", None),
        ),
        out_specs=(P("mix", "row", None, None), P()),
        check_vma=False,
    )
```

```python
import math

import jax
import jax.numpy as jnp
from jax import lax
from jax.experimental import pallas as pl
from jax.experimental.pallas import tpu as pltpu
from jax.sharding import PartitionSpec as P

MESH_AXES = ("row", "mix")
ROWS = 8
VMEM = pl.BlockSpec(memory_space=pltpu.VMEM)


def xor_route(count, bits):
    return [(i, i ^ bits) for i in range(count) if i ^ bits < count]


def turn_route(count, steps):
    return [(i, (i + steps) % count) for i in range(count)]


def neighbours(first, last, axis):
    size = lax.axis_size(axis)
    up = [(i, i + 1) for i in range(size - 1)]
    down = [(i + 1, i) for i in range(size - 1)]
    return lax.ppermute(last, axis, up), lax.ppermute(first, axis, down)


def curl(field_b):
    plane = field_b[:, :, 0]
    below, above = neighbours(plane[:, :2], plane[:, :2], "mix")
    left, right = neighbours(plane[:, 1:, :1], plane[:, 1:, -1:], "row")
    with_rims = jnp.concatenate([left, plane[:, 1:], right], axis=2).astype(jnp.float32)
    center = plane.astype(jnp.float32)
    over_z = (above.astype(jnp.float32) - below.astype(jnp.float32)) * 0.5
    over_x = (with_rims[:, :, 2:] - with_rims[:, :, :-2]) * 0.5
    wide = jnp.pad(center, ((0, 0), (0, 0), (0, 0), (1, 1)))
    over_y = (wide[..., 2:] - wide[..., :-2]) * 0.5
    current_x = over_y[:, 2] - over_z[:, 1]
    current_y = over_z[:, 0] - over_x[:, 1]
    current_z = over_x[:, 0] - over_y[:, 0]
    return jnp.stack([current_x, current_y, current_z], axis=1).astype(jnp.bfloat16)


def parity_sign(a, b):
    both = jnp.bitwise_and(a, b)
    return 1.0 - 2.0 * (lax.population_count(both) % 2).astype(jnp.float32)


def sampled_mixing(velocity, current, test_matrix, signs, sample_index):
    planes = lax.axis_size("mix")
    mine = lax.axis_index("mix")
    core = mine % 2
    hops = range(2, planes, 2)
    wanted = [sample_index] + [lax.ppermute(sample_index, "mix", xor_route(planes, k)) for k in hops]
    wanted = jnp.stack(wanted)
    snaps = velocity.shape[0]
    points = signs.shape[0]

    def flat(part):
        return part.reshape(3 * snaps, points) * signs

    by_part = test_matrix.reshape(snaps, 6, -1)
    for_velocity = by_part[:, :3].reshape(3 * snaps, -1)
    for_current = by_part[:, 3:].reshape(3 * snaps, -1)
    own_sign = (1 - 2 * core).astype(jnp.bfloat16)
    chosen = (wanted[:, None, :] == jnp.arange(points, dtype=jnp.int32)[None, :, None]).astype(jnp.bfloat16)

    def part_sum(part, matrix):
        own = flat(part)
        other = lax.ppermute(own, "mix", xor_route(planes, 1))
        both = jnp.concatenate([own, other])
        gathered = jnp.einsum("sp,tpk->tsk", both, chosen, preferred_element_type=jnp.float32).astype(jnp.bfloat16)
        twice = jnp.concatenate([own_sign * matrix, matrix])
        return jnp.einsum("sj,tsk->tjk", twice, gathered, preferred_element_type=jnp.float32)

    parts = part_sum(velocity, for_velocity) + part_sum(current, for_current)
    total = parity_sign(mine, mine - core) * parts[0]
    for slot, k in enumerate(hops):
        arrived = lax.ppermute(parts[slot + 1], "mix", xor_route(planes, k))
        total = total + parity_sign(mine, (mine ^ k) - core) * arrived
    return total * (1.0 / math.sqrt(6 * snaps) / math.sqrt(planes))


def whole_mixing(velocity, current, test_matrix, signs, sample_index):
    planes = lax.axis_size("mix")
    mine = lax.axis_index("mix")
    snaps = velocity.shape[0]
    snapshot = jnp.concatenate([velocity, current], axis=1).reshape(6 * snaps, -1) * signs
    values = lax.dot_general(
        snapshot, test_matrix, (((0,), (0,)), ((), ())), preferred_element_type=jnp.float32
    ) * (1.0 / math.sqrt(6 * snaps))
    for level in range(planes.bit_length() - 1):
        partner = lax.ppermute(values, "mix", xor_route(planes, 1 << level))
        upper_bit = mine // (1 << level) % 2
        values = jnp.where(upper_bit == 1, partner - values, values + partner)
    return jnp.take(values / math.sqrt(planes), sample_index, axis=0).T


def sum_over_mesh(gram):
    planes, blocks = lax.axis_size("mix"), lax.axis_size("row")
    if planes > 8 or blocks > 4:
        return lax.psum(gram, MESH_AXES)
    n = gram.shape[0]
    core = lax.axis_index("mix") % 2
    low, high = gram[: n // 2], gram[n // 2 :]
    half = jnp.where(core == 0, low, high)
    half = half + lax.ppermute(jnp.where(core == 0, high, low), "mix", xor_route(planes, 1))
    half = half + sum(lax.ppermute(half, "mix", xor_route(planes, k)) for k in range(2, planes, 2))
    half = half + sum(lax.ppermute(half, "row", turn_route(blocks, k)) for k in range(1, blocks))
    other = lax.ppermute(half, "mix", xor_route(planes, 1))
    return jnp.concatenate([jnp.where(core == 0, half, other), jnp.where(core == 0, other, half)])


def product(a, b, dims):
    return lax.dot_general(
        a, b, (dims, ((), ())), precision=lax.Precision.HIGHEST, preferred_element_type=jnp.float32
    )


def eliminate(a_ref, z_ref):
    n = a_ref.shape[0]
    row = lax.broadcasted_iota(jnp.int32, (ROWS, n), 0)
    lane = lax.broadcasted_iota(jnp.int32, (ROWS, n), 1)

    def spread(x):
        return jnp.broadcast_to(x, (ROWS, n))

    def rows_of(ref, start):
        return ref[start : start + ROWS, :]

    for start in range(0, n, ROWS):
        z_ref[start : start + ROWS, :] = jnp.where(lane == row + start, 1.0, 0.0)
    for start in range(0, n, ROWS):
        block, block_z = rows_of(a_ref, start), rows_of(z_ref, start)
        columns = [spread(block[:, start + c : start + c + 1]) for c in range(ROWS)]
        pivots = {(k, c): spread(columns[c][k : k + 1, :]) for c in range(ROWS) for k in range(c + 1)}
        top = [spread(block[k : k + 1, :]) for k in range(ROWS)]
        top_z = [spread(block_z[k : k + 1, :]) for k in range(ROWS)]
        inverse = []
        for k in range(ROWS):
            inverse.append(1.0 / pivots[k, k])
            for i in range(k + 1, ROWS):
                times = pivots[k, i] * inverse[k]
                for c in range(i, ROWS):
                    pivots[i, c] = pivots[i, c] - times * pivots[k, c]
                top[i] = top[i] - times * top[k]
                top_z[i] = top_z[i] - times * top_z[k]
        for below in range(start + ROWS, n, ROWS):
            rest, rest_z = rows_of(a_ref, below), rows_of(z_ref, below)
            columns = [spread(rest[:, start + c : start + c + 1]) for c in range(ROWS)]
            for k in range(ROWS):
                times = columns[k] * inverse[k]
                for c in range(k + 1, ROWS):
                    columns[c] = columns[c] - times * pivots[k, c]
                rest = rest - times * top[k]
                rest_z = rest_z - times * top_z[k]
            a_ref[below : below + ROWS, :] = rest
            z_ref[below : below + ROWS, :] = rest_z
        done, done_z = jnp.zeros_like(block), jnp.zeros_like(block)
        for k in range(ROWS):
            scale = lax.rsqrt(pivots[k, k])
            done = jnp.where(row == k, top[k] * scale, done)
            done_z = jnp.where(row == k, top_z[k] * scale, done_z)
        a_ref[start : start + ROWS, :] = jnp.where(lane >= row + start, done, 0.0)
        z_ref[start : start + ROWS, :] = done_z


def finish_kernel(gram_ref, picked_ref, basis_ref, factor_ref, a_ref, first_ref, second_ref):
    half = a_ref.shape[0]
    nn, nt = ((1,), (0,)), ((1,), (1,))
    a_ref[...] = gram_ref[:half, :half]
    eliminate(a_ref, first_ref)
    first = first_ref[...]
    across = product(first, gram_ref[:half, half:], nn)
    down = product(gram_ref[half:, :half], first, nt)
    factor_ref[:half, :half] = a_ref[...]
    factor_ref[:half, half:] = across
    factor_ref[half:, :half] = jnp.zeros_like(across)
    a_ref[...] = gram_ref[half:, half:] - product(down, across, nn)
    solved = product(picked_ref[:, :half], first, nt)
    basis_ref[:, :half] = solved
    left_over = picked_ref[:, half:] - product(solved, across, nn)
    eliminate(a_ref, second_ref)
    basis_ref[:, half:] = product(left_over, second_ref[...], nt)
    factor_ref[half:, half:] = a_ref[...]


def finish(gram, picked):
    n = gram.shape[0]
    return pl.pallas_call(
        finish_kernel,
        out_shape=(jax.ShapeDtypeStruct(picked.shape, jnp.float32), jax.ShapeDtypeStruct(gram.shape, jnp.float32)),
        in_specs=[VMEM] * 2,
        out_specs=[VMEM] * 2,
        scratch_shapes=[pltpu.VMEM((n // 2, n // 2), jnp.float32)] * 3,
        name="finish",
    )(gram, picked)


def on_device(velocity, field_b, test_signs, row_signs, sample_index):
    snaps = field_b.shape[0]
    sketch_width = test_signs.shape[1]
    planes, blocks = lax.axis_size("mix"), lax.axis_size("row")
    samples = sample_index.shape[-1]
    points = row_signs.size
    test_matrix = (2 * test_signs - 1).astype(jnp.bfloat16)
    signs = (2 * row_signs - 1).astype(jnp.bfloat16).reshape(-1)
    current = curl(field_b)
    sampled_bytes = (planes // 2 - 1) * samples * sketch_width
    whole_bytes = (planes.bit_length() - 1) * points * sketch_width
    mixing = sampled_mixing if sampled_bytes < whole_bytes else whole_mixing
    picked = mixing(velocity[:, :, 0], current, test_matrix, signs, sample_index.reshape(-1))
    gram = jnp.einsum(
        "ik,jk->ij", picked, picked, precision=lax.Precision.HIGHEST, preferred_element_type=jnp.float32
    ) * (1.0 / (planes * blocks * samples))
    basis_rows, factor = finish(sum_over_mesh(gram), picked.T)
    return basis_rows.reshape(sample_index.shape + (sketch_width,)), factor


def solution(mesh):
    return jax.shard_map(
        on_device,
        mesh=mesh,
        in_specs=(
            P(None, None, "mix", "row", None),
            P(None, None, "mix", "row", None),
            P(),
            P("mix", "row", None),
            P("mix", "row", None),
        ),
        out_specs=(P("mix", "row", None, None), P()),
        check_vma=False,
    )
```

```python
import math

import jax
import jax.numpy as jnp
from jax import lax
from jax.experimental import pallas as pl
from jax.experimental.pallas import tpu as pltpu
from jax.sharding import PartitionSpec as P

MESH_AXES = ("row", "mix")
ROWS = 8
LANES = 128
NN, NT, TN = ((1,), (0,)), ((1,), (1,)), ((0,), (0,))
SMEM = pl.BlockSpec(memory_space=pltpu.SMEM)
VMEM = pl.BlockSpec(memory_space=pltpu.VMEM)


def xor_route(count, bits):
    return [(i, i ^ bits) for i in range(count) if i ^ bits < count]


def pair_route(count, first):
    lows = range(first, count - 1, 2)
    return [(i, i + 1) for i in lows] + [(i + 1, i) for i in lows]


def local(kernel, inputs, shapes, scratch=(), megabytes=8, scalars=1):
    return pl.pallas_call(
        kernel,
        out_shape=[jax.ShapeDtypeStruct(shape, dtype) for shape, dtype in shapes],
        in_specs=[SMEM] * scalars + [VMEM] * (len(inputs) - scalars),
        out_specs=[VMEM] * len(shapes),
        scratch_shapes=[pltpu.VMEM(shape, jnp.float32) for shape in scratch],
        compiler_params=pltpu.CompilerParams(vmem_limit_bytes=megabytes << 20),
        name=kernel.__name__,
    )(*inputs)


def lanes_of(ref, x, width):
    return ref[:, x * width : (x + 1) * width]


def to_lanes(source_ref, held_ref, sems, wide_ref, out_ref, signs_ref=None):
    snaps, parts, depth, width = source_ref.shape
    pieces = sems.shape[0]
    step = snaps // pieces
    copies = [
        pltpu.make_async_copy(
            source_ref.at[i * step : (i + 1) * step], held_ref.at[i * step : (i + 1) * step], sems.at[i]
        )
        for i in range(pieces)
    ]
    for copy in copies:
        copy.start()
    tall = step * parts * depth
    for i, copy in enumerate(copies):
        copy.wait()
        values = held_ref[i * step : (i + 1) * step].astype(jnp.float32).reshape(tall, width)
        wide_ref[i * tall : (i + 1) * tall, :] = values
        for c in range(parts):
            for x in range(depth):
                piece = wide_ref[pl.ds(i * tall + c * depth + x, step, stride=parts * depth), :]
                if signs_ref is not None:
                    piece = piece * (2 * signs_ref[x : x + 1, :] - 1).astype(jnp.float32)
                low = c * snaps + i * step
                out_ref[low : low + step, x * width : (x + 1) * width] = piece.astype(out_ref.dtype)


def field_kernel(flags_ref, field_ref, lanes_ref, flat_ref, rim_a_ref, rim_b_ref, held_ref, wide_ref, sems):
    snaps, _, depth, width = field_ref.shape
    to_lanes(field_ref, held_ref, sems, wide_ref, lanes_ref)
    flat_ref[...] = lanes_ref[: 2 * snaps, :]
    odd = flags_ref[1] == 1
    first = lanes_ref[snaps:, :width].astype(jnp.float32)
    last = lanes_ref[snaps:, (depth - 1) * width :].astype(jnp.float32)
    rim_a_ref[...] = jnp.where(odd, first, last).astype(rim_a_ref.dtype)
    rim_b_ref[...] = jnp.where(odd, last, first).astype(rim_b_ref.dtype)


def velocity_kernel(
    flags_ref,
    velocity_ref,
    test_ref,
    signs_ref,
    pair_ref,
    matrix_ref,
    held_ref,
    wide_ref,
    sems,
    bits_ref,
    bits_sem,
    held_signs_ref,
    signs_sem,
):
    snaps, parts = velocity_ref.shape[:2]
    copy_signs = pltpu.make_async_copy(signs_ref, held_signs_ref, signs_sem)
    copy_signs.start()
    copy = pltpu.make_async_copy(test_ref, bits_ref, bits_sem)
    copy.start()
    copy_signs.wait()
    to_lanes(velocity_ref, held_ref, sems, wide_ref, pair_ref, held_signs_ref)
    copy.wait()
    columns = bits_ref.shape[0]
    width = wide_ref.shape[1]
    for low in range(0, bits_ref.shape[1], width):
        wide_ref[:columns, :] = (2 * bits_ref[:, low : low + width] - 1).astype(jnp.float32)
        for c in range(2 * parts):
            piece = wide_ref[pl.ds(c, snaps, stride=2 * parts), :]
            matrix_ref[c * snaps : (c + 1) * snaps, low : low + width] = piece.astype(matrix_ref.dtype)


def relay(kernel, flags, inputs, in_vmem, shapes, scratch=()):
    snaps, parts, depth, width = inputs[0].shape
    held = [pltpu.VMEM(inputs[0].shape, inputs[0].dtype), pltpu.VMEM((snaps * parts * depth, width), jnp.float32)]
    return pl.pallas_call(
        kernel,
        out_shape=[jax.ShapeDtypeStruct(shape, dtype) for shape, dtype in shapes],
        in_specs=[SMEM] + [pl.BlockSpec(memory_space=pl.ANY)] * len(inputs) + [VMEM] * len(in_vmem),
        out_specs=[VMEM] * len(shapes),
        scratch_shapes=held + [pltpu.SemaphoreType.DMA((4,))] + list(scratch),
        compiler_params=pltpu.CompilerParams(vmem_limit_bytes=8 << 20),
        name=kernel.__name__,
    )(flags, *[pltpu.with_memory_space_constraint(array, pltpu.HBM) for array in inputs], *in_vmem)


def curl_kernel(flags_ref, field_ref, plane_a_ref, plane_b_ref, rim_a_ref, rim_b_ref, signs_ref, current_ref):
    snaps = rim_a_ref.shape[0] // 2
    width = rim_a_ref.shape[1]
    depth = field_ref.shape[1] // width
    upward = 0.5 - flags_ref[0].astype(jnp.float32)
    odd_block = flags_ref[1] == 1
    lane = lax.broadcasted_iota(jnp.int32, (snaps, width), 1)

    def field(c, x):
        return lanes_of(field_ref.at[c * snaps : (c + 1) * snaps], x, width).astype(jnp.float32)

    def over_x(c, x):
        rim_a = rim_a_ref[(c - 1) * snaps : c * snaps, :].astype(jnp.float32)
        rim_b = rim_b_ref[(c - 1) * snaps : c * snaps, :].astype(jnp.float32)
        low = field(c, x - 1) if x else jnp.where(odd_block, rim_a, rim_b)
        high = field(c, x + 1) if x < depth - 1 else jnp.where(odd_block, rim_b, rim_a)
        return (high - low) * 0.5

    def over_y(c, x):
        values = field(c, x)
        low = jnp.where(lane == 0, 0.0, pltpu.roll(values, 1, 1))
        high = jnp.where(lane == width - 1, 0.0, pltpu.roll(values, width - 1, 1))
        return (high - low) * 0.5

    def over_z(c, x):
        a = lanes_of(plane_a_ref.at[c * snaps : (c + 1) * snaps], x, width).astype(jnp.float32)
        b = lanes_of(plane_b_ref.at[c * snaps : (c + 1) * snaps], x, width).astype(jnp.float32)
        return (a - b) * upward

    for x in range(depth):
        sign = (2 * signs_ref[x : x + 1, :] - 1).astype(jnp.float32)
        current = (
            over_y(2, x) - over_z(1, x),
            over_z(0, x) - over_x(2, x),
            over_x(1, x) - over_y(0, x),
        )
        for c, values in enumerate(current):
            current_ref[c * snaps : (c + 1) * snaps, x * width : (x + 1) * width] = (values * sign).astype(
                current_ref.dtype
            )


def parts_kernel(flags_ref, wanted_ref, pair_ref, other_ref, current_ref, other_current_ref, matrix_ref, *refs):
    part_refs, held_ref = refs[:-1], refs[-1]
    rows, points = current_ref.shape
    width = held_ref.shape[1]
    halves = matrix_ref.shape[1] // width
    own_sign = (1 - 2 * flags_ref[0]).astype(jnp.float32)

    def sketch(values_ref, matrix):
        return lax.dot_general(values_ref, matrix, (TN, ((), ())), preferred_element_type=jnp.float32)

    plain = matrix_ref[...]
    turned = (plain.astype(jnp.float32) * own_sign).astype(plain.dtype)
    total = sketch(pair_ref[-rows:, :], turned[:rows]) + sketch(other_ref[-rows:, :], plain[:rows])
    total = total + sketch(current_ref[...], turned[rows:]) + sketch(other_current_ref[...], plain[rows:])
    for half in range(halves):
        held_ref[pl.ds(half, points, stride=halves), :] = total[:, half * width : (half + 1) * width]
    samples = part_refs[0].shape[0] // halves
    batch = 16
    for slot, part_ref in enumerate(part_refs):
        for first in range(0, samples, batch):
            at = [pl.multiple_of(wanted_ref[slot * samples + first + i], halves) for i in range(batch)]
            values = [held_ref[pl.ds(start, halves), :] for start in at]
            for i in range(batch):
                part_ref[(first + i) * halves : (first + i + 1) * halves, :] = values[i]


def gram_kernel(signs_ref, *refs):
    parts, (picked_ref, packed_ref, held_ref) = refs[:-3], refs[-3:]
    total = signs_ref[0] * parts[0][...]
    for slot in range(1, len(parts)):
        total = total + signs_ref[slot] * parts[slot][...]
    held_ref[...] = total
    samples, wide = picked_ref.shape
    width = held_ref.shape[1]
    halves = wide // width
    picked = [held_ref[pl.ds(half, samples, stride=halves), :] for half in range(halves)]
    picked = jnp.concatenate(picked, axis=1)
    picked_ref[...] = picked
    pack(product(picked.T, picked, NN) * signs_ref[len(parts)], packed_ref)


def product(a, b, dims):
    return lax.dot_general(
        a, b, (dims, ((), ())), precision=lax.Precision.HIGHEST, preferred_element_type=jnp.float32
    )


def eliminate(a_ref, z_ref):
    n = a_ref.shape[0]
    row = lax.broadcasted_iota(jnp.int32, (ROWS, n), 0)
    lane = lax.broadcasted_iota(jnp.int32, (ROWS, n), 1)

    def spread(x):
        return jnp.broadcast_to(x, (ROWS, n))

    def rows_of(ref, start):
        return ref[start : start + ROWS, :]

    for start in range(0, n, ROWS):
        z_ref[start : start + ROWS, :] = jnp.where(lane == row + start, 1.0, 0.0)
    for start in range(0, n, ROWS):
        block, block_z = rows_of(a_ref, start), rows_of(z_ref, start)
        columns = [spread(block[:, start + c : start + c + 1]) for c in range(ROWS)]
        pivots = {(k, c): spread(columns[c][k : k + 1, :]) for c in range(ROWS) for k in range(c + 1)}
        top = [spread(block[k : k + 1, :]) for k in range(ROWS)]
        top_z = [spread(block_z[k : k + 1, :]) for k in range(ROWS)]
        inverse = []
        for k in range(ROWS):
            inverse.append(1.0 / pivots[k, k])
            for i in range(k + 1, ROWS):
                times = pivots[k, i] * inverse[k]
                for c in range(i, ROWS):
                    pivots[i, c] = pivots[i, c] - times * pivots[k, c]
                top[i] = top[i] - times * top[k]
                top_z[i] = top_z[i] - times * top_z[k]
        for below in range(start + ROWS, n, ROWS):
            rest, rest_z = rows_of(a_ref, below), rows_of(z_ref, below)
            columns = [spread(rest[:, start + c : start + c + 1]) for c in range(ROWS)]
            for k in range(ROWS):
                times = columns[k] * inverse[k]
                for c in range(k + 1, ROWS):
                    columns[c] = columns[c] - times * pivots[k, c]
                rest = rest - times * top[k]
                rest_z = rest_z - times * top_z[k]
            a_ref[below : below + ROWS, :] = rest
            z_ref[below : below + ROWS, :] = rest_z
        done, done_z = jnp.zeros_like(block), jnp.zeros_like(block)
        for k in range(ROWS):
            scale = lax.rsqrt(pivots[k, k])
            done = jnp.where(row == k, top[k] * scale, done)
            done_z = jnp.where(row == k, top_z[k] * scale, done_z)
        a_ref[start : start + ROWS, :] = jnp.where(lane >= row + start, done, 0.0)
        z_ref[start : start + ROWS, :] = done_z


def pack(gram, packed_ref):
    n = gram.shape[0]
    q, h = n // 4, n // 2
    lane = lax.broadcasted_iota(jnp.int32, (q, h), 1)
    packed_ref[:q, :] = gram[:q, :]
    packed_ref[q:h, :h] = jnp.where(lane < q, gram[h : h + q, h:], gram[q:h, :h])
    packed_ref[q:h, h:] = gram[q:h, h:]
    packed_ref[h:, :h] = gram[h + q : h + q + q // 2, h:]
    packed_ref[h:, h:] = gram[h + q + q // 2 :, h:]


def unpack(packed):
    n = packed.shape[1]
    q, h = n // 4, n // 2
    row = lax.broadcasted_iota(jnp.int32, (h, h), 0)
    lane = lax.broadcasted_iota(jnp.int32, (h, h), 1)
    top = packed[:h, :h]
    first = jnp.where((row >= q) & (lane < q), top.T, top)
    bottom = jnp.concatenate([packed[q:h, :h], packed[h:, :h], packed[h:, h:]])
    last = jnp.where((row < q) & (lane >= q), bottom.T, bottom)
    return first, packed[:h, h:], last


def parity_sign(a, b):
    both = jnp.bitwise_and(a, b)
    return 1.0 - 2.0 * (lax.population_count(both) % 2).astype(jnp.float32)


def doubled(rows, bit):
    return jnp.concatenate([rows, lax.ppermute(rows, "mix", xor_route(lax.axis_size("mix"), bit))])


def sampled_mixing(flags, pair, other, current, matrix, wanted):
    planes = lax.axis_size("mix")
    mine = lax.axis_index("mix")
    targets, samples = wanted.shape
    halves = matrix.shape[1] // LANES
    part = ((samples * halves, LANES), jnp.float32)
    other_current = lax.ppermute(current, "mix", xor_route(planes, 1))
    inputs = (flags, wanted.reshape(-1) * halves, pair, other, current, other_current, matrix)
    scratch = ((current.shape[1] * halves, LANES),)
    parts = local(parts_kernel, inputs, [part] * targets, scratch, megabytes=12, scalars=2)
    hops = range(2, planes, 2)
    arrived = [parts[0]] + [lax.ppermute(part, "mix", xor_route(planes, k)) for part, k in zip(parts[1:], hops)]
    return arrived, [parity_sign(mine, (mine ^ k) - mine % 2) for k in range(0, planes, 2)]


def whole_mixing(pair, current, matrix, wanted):
    planes = lax.axis_size("mix")
    mine = lax.axis_index("mix")
    snapshot = jnp.concatenate([pair[-current.shape[0] :], current])
    values = lax.dot_general(snapshot, matrix, (((0,), (0,)), ((), ())), preferred_element_type=jnp.float32)
    for level in range(planes.bit_length() - 1):
        partner = lax.ppermute(values, "mix", xor_route(planes, 1 << level))
        upper_bit = mine // (1 << level) % 2
        values = jnp.where(upper_bit == 1, partner - values, values + partner)
    return [jnp.take(values, wanted[0], axis=0).reshape(-1, LANES)], [jnp.float32(1.0)]


def sum_over_mesh(packed):
    planes, blocks = lax.axis_size("mix"), lax.axis_size("row")
    half_rows = packed.shape[0] // 2
    low, high = packed[:half_rows], packed[half_rows:]
    if planes > 8 or blocks != 4:
        low, high = lax.psum((low, high), MESH_AXES)
        return low, high, jnp.int32(0)
    core = lax.axis_index("mix") % 2
    half = jnp.where(core == 0, low, high)
    half = half + lax.ppermute(jnp.where(core == 0, high, low), "mix", xor_route(planes, 1))
    half = half + sum(lax.ppermute(half, "mix", xor_route(planes, k)) for k in range(2, planes, 2))
    half = half + sum(lax.ppermute(half, "row", xor_route(blocks, k)) for k in range(1, blocks))
    return half, lax.ppermute(half, "mix", xor_route(planes, 1)), core


def finish_kernel(core_ref, half_ref, other_ref, picked_ref, basis_ref, factor_ref, a_ref, first_ref, second_ref):
    side = a_ref.shape[0]
    half, other = half_ref[...], other_ref[...]
    swap = core_ref[0] != 0
    packed = jnp.concatenate([jnp.where(swap, other, half), jnp.where(swap, half, other)])
    corner, right, last = unpack(packed)
    a_ref[...] = corner
    eliminate(a_ref, first_ref)
    first = first_ref[...]
    across = product(first, right, NN)
    down = product(right.T, first, NT)
    factor_ref[:side, :side] = a_ref[...]
    factor_ref[:side, side:] = across
    factor_ref[side:, :side] = jnp.zeros_like(across)
    a_ref[...] = last - product(down, across, NN)
    solved = product(picked_ref[:, :side], first, NT)
    basis_ref[:, :side] = solved
    left_over = picked_ref[:, side:] - product(solved, across, NN)
    eliminate(a_ref, second_ref)
    basis_ref[:, side:] = product(left_over, second_ref[...], NT)
    factor_ref[side:, side:] = a_ref[...]


def finish(half, other, core, picked):
    n = picked.shape[1]
    shapes = [(picked.shape, jnp.float32), ((n, n), jnp.float32)]
    scratch = ((n // 2, n // 2),) * 3
    return local(finish_kernel, (core.reshape(1), half, other, picked), shapes, scratch)


def on_device(velocity, field_b, test_signs, row_signs, sample_index):
    snaps, parts, _, depth, width = field_b.shape
    sketch_width = test_signs.shape[1]
    planes, blocks = lax.axis_size("mix"), lax.axis_size("row")
    samples = sample_index.shape[-1]
    points = depth * width
    flags = jnp.stack([lax.axis_index("mix") % 2, lax.axis_index("row") % 2]).astype(jnp.int32)
    signs = row_signs[0]
    lanes = ((parts * snaps, points), jnp.bfloat16)
    flat = ((2 * snaps, points), jnp.bfloat16)
    rim = ((2 * snaps, width), jnp.bfloat16)
    sampled_bytes = (planes // 2 - 1) * samples * sketch_width
    whole_bytes = (planes.bit_length() - 1) * points * sketch_width
    sampled = sampled_bytes < whole_bytes
    wanted = sample_index.reshape(1, -1)
    if sampled:
        wanted = doubled(wanted, 2)
    field, flat, rim_a, rim_b = relay(field_kernel, flags, [field_b[:, :, 0]], [], [lanes, flat, rim, rim])
    plane_b = lax.ppermute(flat, "mix", pair_route(planes, 1))
    rim_a = lax.ppermute(rim_a, "row", pair_route(blocks, 0))
    rim_b = lax.ppermute(rim_b, "row", pair_route(blocks, 1))
    matrix = ((2 * parts * snaps, sketch_width), jnp.bfloat16)
    scratch = [pltpu.VMEM(test_signs.shape, jnp.int32), pltpu.SemaphoreType.DMA]
    scratch += [pltpu.VMEM(signs.shape, jnp.int32), pltpu.SemaphoreType.DMA]
    inputs = [velocity[:, :, 0], test_signs, signs]
    pair, matrix = relay(velocity_kernel, flags, inputs, [], [lanes, matrix], scratch)
    plane_a = lax.ppermute(flat, "mix", pair_route(planes, 0))
    pair, wanted = lax.optimization_barrier((pair, wanted))
    other = lax.ppermute(pair, "mix", pair_route(planes, 0))
    if sampled:
        for level in range(2, planes.bit_length() - 1):
            wanted = doubled(wanted, 1 << level)
    (current,) = local(curl_kernel, (flags, field, plane_a, plane_b, rim_a, rim_b, signs), [lanes])
    if sampled:
        added, part_signs = sampled_mixing(flags, pair, other, current, matrix, wanted)
    else:
        added, part_signs = whole_mixing(pair, current, matrix, wanted)
    scale = 1.0 / math.sqrt(6 * snaps * planes)
    factors = jnp.stack([sign * scale for sign in part_signs] + [jnp.float32(1.0 / (planes * blocks * samples))])
    picked, packed = local(
        gram_kernel,
        (factors, *added),
        [((samples, sketch_width), jnp.float32), ((sketch_width * 5 // 8, sketch_width), jnp.float32)],
        (added[0].shape,),
    )
    basis_rows, factor = finish(*sum_over_mesh(packed), picked)
    return basis_rows.reshape(sample_index.shape + (sketch_width,)), factor


def solution(mesh):
    return jax.shard_map(
        on_device,
        mesh=mesh,
        in_specs=(
            P(None, None, "mix", "row", None),
            P(None, None, "mix", "row", None),
            P(),
            P("mix", "row", None),
            P("mix", "row", None),
        ),
        out_specs=(P("mix", "row", None, None), P()),
        check_vma=False,
    )
```

```python
import math

import jax
import jax.numpy as jnp
from jax import lax
from jax.experimental import pallas as pl
from jax.experimental.pallas import tpu as pltpu
from jax.sharding import PartitionSpec as P

MESH_AXES = ("row", "mix")
ROWS = 8
LANES = 128
NN, NT, TN = ((1,), (0,)), ((1,), (1,)), ((0,), (0,))
SMEM = pl.BlockSpec(memory_space=pltpu.SMEM)
VMEM = pl.BlockSpec(memory_space=pltpu.VMEM)


def xor_route(count, bits):
    return [(i, i ^ bits) for i in range(count) if i ^ bits < count]


def pair_route(count, first):
    lows = range(first, count - 1, 2)
    return [(i, i + 1) for i in lows] + [(i + 1, i) for i in lows]


def local(kernel, inputs, shapes, scratch=(), megabytes=8, scalars=1):
    return pl.pallas_call(
        kernel,
        out_shape=[jax.ShapeDtypeStruct(shape, dtype) for shape, dtype in shapes],
        in_specs=[SMEM] * scalars + [VMEM] * (len(inputs) - scalars),
        out_specs=[VMEM] * len(shapes),
        scratch_shapes=[pltpu.VMEM(shape, jnp.float32) for shape in scratch],
        compiler_params=pltpu.CompilerParams(vmem_limit_bytes=megabytes << 20),
        name=kernel.__name__,
    )(*inputs)


def lanes_of(ref, x, width):
    return ref[:, x * width : (x + 1) * width]


def to_lanes(source_ref, held_ref, sems, wide_ref, out_ref, signs_ref=None):
    snaps, parts, depth, width = source_ref.shape
    pieces = sems.shape[0]
    step = snaps // pieces
    copies = [
        pltpu.make_async_copy(
            source_ref.at[i * step : (i + 1) * step], held_ref.at[i * step : (i + 1) * step], sems.at[i]
        )
        for i in range(pieces)
    ]
    for copy in copies:
        copy.start()
    tall = step * parts * depth
    for i, copy in enumerate(copies):
        copy.wait()
        values = held_ref[i * step : (i + 1) * step].astype(jnp.float32).reshape(tall, width)
        wide_ref[i * tall : (i + 1) * tall, :] = values
        for c in range(parts):
            for x in range(depth):
                piece = wide_ref[pl.ds(i * tall + c * depth + x, step, stride=parts * depth), :]
                if signs_ref is not None:
                    piece = piece * (2 * signs_ref[x : x + 1, :] - 1).astype(jnp.float32)
                low = c * snaps + i * step
                out_ref[low : low + step, x * width : (x + 1) * width] = piece.astype(out_ref.dtype)


def field_kernel(flags_ref, field_ref, lanes_ref, flat_ref, rim_a_ref, rim_b_ref, held_ref, wide_ref, sems):
    snaps, _, depth, width = field_ref.shape
    to_lanes(field_ref, held_ref, sems, wide_ref, lanes_ref)
    flat_ref[...] = lanes_ref[: 2 * snaps, :]
    odd = flags_ref[1] == 1
    first = lanes_ref[snaps:, :width].astype(jnp.float32)
    last = lanes_ref[snaps:, (depth - 1) * width :].astype(jnp.float32)
    rim_a_ref[...] = jnp.where(odd, first, last).astype(rim_a_ref.dtype)
    rim_b_ref[...] = jnp.where(odd, last, first).astype(rim_b_ref.dtype)


def velocity_kernel(
    flags_ref,
    velocity_ref,
    test_ref,
    signs_ref,
    pair_ref,
    matrix_ref,
    held_ref,
    wide_ref,
    sems,
    bits_ref,
    bits_sem,
    held_signs_ref,
    signs_sem,
):
    snaps, parts = velocity_ref.shape[:2]
    copy_signs = pltpu.make_async_copy(signs_ref, held_signs_ref, signs_sem)
    copy_signs.start()
    copy = pltpu.make_async_copy(test_ref, bits_ref, bits_sem)
    copy.start()
    copy_signs.wait()
    to_lanes(velocity_ref, held_ref, sems, wide_ref, pair_ref, held_signs_ref)
    copy.wait()
    columns = bits_ref.shape[0]
    width = wide_ref.shape[1]
    for low in range(0, bits_ref.shape[1], width):
        wide_ref[:columns, :] = (2 * bits_ref[:, low : low + width] - 1).astype(jnp.float32)
        for c in range(2 * parts):
            piece = wide_ref[pl.ds(c, snaps, stride=2 * parts), :]
            matrix_ref[c * snaps : (c + 1) * snaps, low : low + width] = piece.astype(matrix_ref.dtype)


def relay(kernel, flags, inputs, in_vmem, shapes, scratch=()):
    snaps, parts, depth, width = inputs[0].shape
    held = [pltpu.VMEM(inputs[0].shape, inputs[0].dtype), pltpu.VMEM((snaps * parts * depth, width), jnp.float32)]
    return pl.pallas_call(
        kernel,
        out_shape=[jax.ShapeDtypeStruct(shape, dtype) for shape, dtype in shapes],
        in_specs=[SMEM] + [pl.BlockSpec(memory_space=pl.ANY)] * len(inputs) + [VMEM] * len(in_vmem),
        out_specs=[VMEM] * len(shapes),
        scratch_shapes=held + [pltpu.SemaphoreType.DMA((4,))] + list(scratch),
        compiler_params=pltpu.CompilerParams(vmem_limit_bytes=8 << 20),
        name=kernel.__name__,
    )(flags, *[pltpu.with_memory_space_constraint(array, pltpu.HBM) for array in inputs], *in_vmem)


def curl_kernel(flags_ref, field_ref, plane_a_ref, plane_b_ref, rim_a_ref, rim_b_ref, signs_ref, current_ref):
    snaps = rim_a_ref.shape[0] // 2
    width = rim_a_ref.shape[1]
    depth = field_ref.shape[1] // width
    upward = 0.5 - flags_ref[0].astype(jnp.float32)
    odd_block = flags_ref[1] == 1
    lane = lax.broadcasted_iota(jnp.int32, (snaps, width), 1)

    def field(c, x):
        return lanes_of(field_ref.at[c * snaps : (c + 1) * snaps], x, width).astype(jnp.float32)

    def over_x(c, x):
        rim_a = rim_a_ref[(c - 1) * snaps : c * snaps, :].astype(jnp.float32)
        rim_b = rim_b_ref[(c - 1) * snaps : c * snaps, :].astype(jnp.float32)
        low = field(c, x - 1) if x else jnp.where(odd_block, rim_a, rim_b)
        high = field(c, x + 1) if x < depth - 1 else jnp.where(odd_block, rim_b, rim_a)
        return (high - low) * 0.5

    def over_y(c, x):
        values = field(c, x)
        low = jnp.where(lane == 0, 0.0, pltpu.roll(values, 1, 1))
        high = jnp.where(lane == width - 1, 0.0, pltpu.roll(values, width - 1, 1))
        return (high - low) * 0.5

    def over_z(c, x):
        a = lanes_of(plane_a_ref.at[c * snaps : (c + 1) * snaps], x, width).astype(jnp.float32)
        b = lanes_of(plane_b_ref.at[c * snaps : (c + 1) * snaps], x, width).astype(jnp.float32)
        return (a - b) * upward

    for x in range(depth):
        sign = (2 * signs_ref[x : x + 1, :] - 1).astype(jnp.float32)
        current = (
            over_y(2, x) - over_z(1, x),
            over_z(0, x) - over_x(2, x),
            over_x(1, x) - over_y(0, x),
        )
        for c, values in enumerate(current):
            current_ref[c * snaps : (c + 1) * snaps, x * width : (x + 1) * width] = (values * sign).astype(
                current_ref.dtype
            )


def parts_kernel(flags_ref, wanted_ref, pair_ref, other_ref, current_ref, other_current_ref, matrix_ref, *refs):
    part_refs, held_ref = refs[:-1], refs[-1]
    rows, points = current_ref.shape
    width = held_ref.shape[1]
    halves = matrix_ref.shape[1] // width
    own_sign = (1 - 2 * flags_ref[0]).astype(jnp.float32)

    def sketch(values_ref, matrix):
        return lax.dot_general(values_ref, matrix, (TN, ((), ())), preferred_element_type=jnp.float32)

    plain = matrix_ref[...]
    turned = (plain.astype(jnp.float32) * own_sign).astype(plain.dtype)
    total = sketch(pair_ref[-rows:, :], turned[:rows]) + sketch(other_ref[-rows:, :], plain[:rows])
    total = total + sketch(current_ref[...], turned[rows:]) + sketch(other_current_ref[...], plain[rows:])
    for half in range(halves):
        held_ref[pl.ds(half, points, stride=halves), :] = total[:, half * width : (half + 1) * width]
    samples = part_refs[0].shape[0] // halves
    batch = 16
    for slot, part_ref in enumerate(part_refs):
        for first in range(0, samples, batch):
            at = [pl.multiple_of(wanted_ref[slot * samples + first + i], halves) for i in range(batch)]
            values = [held_ref[pl.ds(start, halves), :] for start in at]
            for i in range(batch):
                part_ref[(first + i) * halves : (first + i + 1) * halves, :] = values[i]


def gram_kernel(signs_ref, *refs):
    parts, (picked_ref, packed_ref, held_ref) = refs[:-3], refs[-3:]
    total = signs_ref[0] * parts[0][...]
    for slot in range(1, len(parts)):
        total = total + signs_ref[slot] * parts[slot][...]
    held_ref[...] = total
    samples, wide = picked_ref.shape
    width = held_ref.shape[1]
    halves = wide // width
    picked = [held_ref[pl.ds(half, samples, stride=halves), :] for half in range(halves)]
    picked = jnp.concatenate(picked, axis=1)
    picked_ref[...] = picked
    pack(product(picked.T, picked, NN) * signs_ref[len(parts)], packed_ref)


def product(a, b, dims):
    return lax.dot_general(
        a, b, (dims, ((), ())), precision=lax.Precision.HIGHEST, preferred_element_type=jnp.float32
    )


def eliminate(a_ref, z_ref):
    n = a_ref.shape[0]
    blocks = n // ROWS
    row = lax.broadcasted_iota(jnp.int32, (ROWS, n), 0)
    lane = lax.broadcasted_iota(jnp.int32, (ROWS, n), 1)

    def spread(x):
        return jnp.broadcast_to(x, (ROWS, n))

    def column(block, c):
        return spread(block[:, c : c + 1])

    def line(block, k):
        return spread(block[k : k + 1, :])

    rest = [a_ref[b * ROWS : (b + 1) * ROWS, :] for b in range(blocks)]
    rest_z = [jnp.where(lane == row + b * ROWS, 1.0, 0.0) for b in range(blocks)]
    columns = [column(rest[0], c) for c in range(ROWS)]
    for b in range(blocks):
        start = b * ROWS
        pivots = {(k, c): line(columns[c], k) for c in range(ROWS) for k in range(c + 1)}
        top = [line(rest[b], k) for k in range(ROWS)]
        top_z = [line(rest_z[b], k) for k in range(ROWS)]
        following = range(b + 1, min(b + 2, blocks))
        for g in following:
            next_old = [column(rest[g], start + c) for c in range(ROWS)]
            columns = [column(rest[g], start + ROWS + c) for c in range(ROWS)]
        inverse = []
        for k in range(ROWS):
            inverse.append(1.0 / pivots[k, k])
            for i in range(k + 1, ROWS):
                times = pivots[k, i] * inverse[k]
                for c in range(i, ROWS):
                    pivots[i, c] = pivots[i, c] - times * pivots[k, c]
                top[i] = top[i] - times * top[k]
                top_z[i] = top_z[i] - times * top_z[k]
            for g in following:
                times = next_old[k] * inverse[k]
                columns = [values - times * line(next_old[k], c) for c, values in enumerate(columns)]
                for c in range(k + 1, ROWS):
                    next_old[c] = next_old[c] - times * pivots[k, c]
                rest[g] = rest[g] - times * top[k]
                rest_z[g] = rest_z[g] - times * top_z[k]
        for g in range(b + 2, blocks):
            old = [column(rest[g], start + c) for c in range(ROWS)]
            for k in range(ROWS):
                times = old[k] * inverse[k]
                for c in range(k + 1, ROWS):
                    old[c] = old[c] - times * pivots[k, c]
                rest[g] = rest[g] - times * top[k]
                rest_z[g] = rest_z[g] - times * top_z[k]
        done, done_z = jnp.zeros((ROWS, n), jnp.float32), jnp.zeros((ROWS, n), jnp.float32)
        for k in range(ROWS):
            scale = lax.rsqrt(pivots[k, k])
            done = jnp.where(row == k, top[k] * scale, done)
            done_z = jnp.where(row == k, top_z[k] * scale, done_z)
        a_ref[start : start + ROWS, :] = jnp.where(lane >= row + start, done, 0.0)
        z_ref[start : start + ROWS, :] = done_z


def pack(gram, packed_ref):
    n = gram.shape[0]
    q, h = n // 4, n // 2
    lane = lax.broadcasted_iota(jnp.int32, (q, h), 1)
    packed_ref[:q, :] = gram[:q, :]
    packed_ref[q:h, :h] = jnp.where(lane < q, gram[h : h + q, h:], gram[q:h, :h])
    packed_ref[q:h, h:] = gram[q:h, h:]
    packed_ref[h:, :h] = gram[h + q : h + q + q // 2, h:]
    packed_ref[h:, h:] = gram[h + q + q // 2 :, h:]


def unpack(packed):
    n = packed.shape[1]
    q, h = n // 4, n // 2
    row = lax.broadcasted_iota(jnp.int32, (h, h), 0)
    lane = lax.broadcasted_iota(jnp.int32, (h, h), 1)
    top = packed[:h, :h]
    first = jnp.where((row >= q) & (lane < q), top.T, top)
    bottom = jnp.concatenate([packed[q:h, :h], packed[h:, :h], packed[h:, h:]])
    last = jnp.where((row < q) & (lane >= q), bottom.T, bottom)
    return first, packed[:h, h:], last


def parity_sign(a, b):
    both = jnp.bitwise_and(a, b)
    return 1.0 - 2.0 * (lax.population_count(both) % 2).astype(jnp.float32)


def doubled(rows, bit):
    return jnp.concatenate([rows, lax.ppermute(rows, "mix", xor_route(lax.axis_size("mix"), bit))])


def sampled_mixing(flags, pair, other, current, matrix, wanted):
    planes = lax.axis_size("mix")
    mine = lax.axis_index("mix")
    targets, samples = wanted.shape
    halves = matrix.shape[1] // LANES
    part = ((samples * halves, LANES), jnp.float32)
    other_current = lax.ppermute(current, "mix", xor_route(planes, 1))
    inputs = (flags, wanted.reshape(-1) * halves, pair, other, current, other_current, matrix)
    scratch = ((current.shape[1] * halves, LANES),)
    parts = local(parts_kernel, inputs, [part] * targets, scratch, megabytes=12, scalars=2)
    hops = range(2, planes, 2)
    arrived = [parts[0]] + [lax.ppermute(part, "mix", xor_route(planes, k)) for part, k in zip(parts[1:], hops)]
    return arrived, [parity_sign(mine, (mine ^ k) - mine % 2) for k in range(0, planes, 2)]


def whole_mixing(pair, current, matrix, wanted):
    planes = lax.axis_size("mix")
    mine = lax.axis_index("mix")
    snapshot = jnp.concatenate([pair[-current.shape[0] :], current])
    values = lax.dot_general(snapshot, matrix, (((0,), (0,)), ((), ())), preferred_element_type=jnp.float32)
    for level in range(planes.bit_length() - 1):
        partner = lax.ppermute(values, "mix", xor_route(planes, 1 << level))
        upper_bit = mine // (1 << level) % 2
        values = jnp.where(upper_bit == 1, partner - values, values + partner)
    return [jnp.take(values, wanted[0], axis=0).reshape(-1, LANES)], [jnp.float32(1.0)]


def sum_over_mesh(packed):
    planes, blocks = lax.axis_size("mix"), lax.axis_size("row")
    half_rows = packed.shape[0] // 2
    low, high = packed[:half_rows], packed[half_rows:]
    if planes > 8 or blocks != 4:
        low, high = lax.psum((low, high), MESH_AXES)
        return low, high, jnp.int32(0)
    core = lax.axis_index("mix") % 2
    half = jnp.where(core == 0, low, high)
    half = half + lax.ppermute(jnp.where(core == 0, high, low), "mix", xor_route(planes, 1))
    half = half + sum(lax.ppermute(half, "mix", xor_route(planes, k)) for k in range(2, planes, 2))
    half = half + sum(lax.ppermute(half, "row", xor_route(blocks, k)) for k in range(1, blocks))
    return half, lax.ppermute(half, "mix", xor_route(planes, 1)), core


def finish_kernel(core_ref, half_ref, other_ref, picked_ref, basis_ref, factor_ref, a_ref, first_ref, second_ref):
    side = a_ref.shape[0]
    half, other = half_ref[...], other_ref[...]
    swap = core_ref[0] != 0
    packed = jnp.concatenate([jnp.where(swap, other, half), jnp.where(swap, half, other)])
    corner, right, last = unpack(packed)
    a_ref[...] = corner
    eliminate(a_ref, first_ref)
    first = first_ref[...]
    across = product(first, right, NN)
    down = product(right.T, first, NT)
    factor_ref[:side, :side] = a_ref[...]
    factor_ref[:side, side:] = across
    factor_ref[side:, :side] = jnp.zeros_like(across)
    a_ref[...] = last - product(down, across, NN)
    solved = product(picked_ref[:, :side], first, NT)
    basis_ref[:, :side] = solved
    left_over = picked_ref[:, side:] - product(solved, across, NN)
    eliminate(a_ref, second_ref)
    basis_ref[:, side:] = product(left_over, second_ref[...], NT)
    factor_ref[side:, side:] = a_ref[...]


def finish(half, other, core, picked):
    n = picked.shape[1]
    shapes = [(picked.shape, jnp.float32), ((n, n), jnp.float32)]
    scratch = ((n // 2, n // 2),) * 3
    return local(finish_kernel, (core.reshape(1), half, other, picked), shapes, scratch)


def on_device(velocity, field_b, test_signs, row_signs, sample_index):
    snaps, parts, _, depth, width = field_b.shape
    sketch_width = test_signs.shape[1]
    planes, blocks = lax.axis_size("mix"), lax.axis_size("row")
    samples = sample_index.shape[-1]
    points = depth * width
    flags = jnp.stack([lax.axis_index("mix") % 2, lax.axis_index("row") % 2]).astype(jnp.int32)
    signs = row_signs[0]
    lanes = ((parts * snaps, points), jnp.bfloat16)
    flat = ((2 * snaps, points), jnp.bfloat16)
    rim = ((2 * snaps, width), jnp.bfloat16)
    sampled_bytes = (planes // 2 - 1) * samples * sketch_width
    whole_bytes = (planes.bit_length() - 1) * points * sketch_width
    sampled = sampled_bytes < whole_bytes
    wanted = sample_index.reshape(1, -1)
    if sampled:
        wanted = doubled(wanted, 2)
    field, flat, rim_a, rim_b = relay(field_kernel, flags, [field_b[:, :, 0]], [], [lanes, flat, rim, rim])
    plane_b = lax.ppermute(flat, "mix", pair_route(planes, 1))
    rim_a = lax.ppermute(rim_a, "row", pair_route(blocks, 0))
    rim_b = lax.ppermute(rim_b, "row", pair_route(blocks, 1))
    matrix = ((2 * parts * snaps, sketch_width), jnp.bfloat16)
    scratch = [pltpu.VMEM(test_signs.shape, jnp.int32), pltpu.SemaphoreType.DMA]
    scratch += [pltpu.VMEM(signs.shape, jnp.int32), pltpu.SemaphoreType.DMA]
    inputs = [velocity[:, :, 0], test_signs, signs]
    pair, matrix = relay(velocity_kernel, flags, inputs, [], [lanes, matrix], scratch)
    plane_a = lax.ppermute(flat, "mix", pair_route(planes, 0))
    pair, wanted = lax.optimization_barrier((pair, wanted))
    other = lax.ppermute(pair, "mix", pair_route(planes, 0))
    if sampled:
        for level in range(2, planes.bit_length() - 1):
            wanted = doubled(wanted, 1 << level)
    (current,) = local(curl_kernel, (flags, field, plane_a, plane_b, rim_a, rim_b, signs), [lanes])
    if sampled:
        added, part_signs = sampled_mixing(flags, pair, other, current, matrix, wanted)
    else:
        added, part_signs = whole_mixing(pair, current, matrix, wanted)
    scale = 1.0 / math.sqrt(6 * snaps * planes)
    factors = jnp.stack([sign * scale for sign in part_signs] + [jnp.float32(1.0 / (planes * blocks * samples))])
    picked, packed = local(
        gram_kernel,
        (factors, *added),
        [((samples, sketch_width), jnp.float32), ((sketch_width * 5 // 8, sketch_width), jnp.float32)],
        (added[0].shape,),
    )
    basis_rows, factor = finish(*sum_over_mesh(packed), picked)
    return basis_rows.reshape(sample_index.shape + (sketch_width,)), factor


def solution(mesh):
    return jax.shard_map(
        on_device,
        mesh=mesh,
        in_specs=(
            P(None, None, "mix", "row", None),
            P(None, None, "mix", "row", None),
            P(),
            P("mix", "row", None),
            P("mix", "row", None),
        ),
        out_specs=(P("mix", "row", None, None), P()),
        check_vma=False,
    )
```

```python
import math

import jax
import jax.numpy as jnp
from jax import lax
from jax.experimental import pallas as pl
from jax.experimental.pallas import tpu as pltpu
from jax.sharding import PartitionSpec as P

MESH_AXES = ("row", "mix")
ROWS = 8
LANES = 128
NEAR = 4
NN, NT, TN = ((1,), (0,)), ((1,), (1,)), ((0,), (0,))
SMEM = pl.BlockSpec(memory_space=pltpu.SMEM)
VMEM = pl.BlockSpec(memory_space=pltpu.VMEM)


def xor_route(count, bits):
    return [(i, i ^ bits) for i in range(count) if i ^ bits < count]


def pair_route(count, first):
    lows = range(first, count - 1, 2)
    return [(i, i + 1) for i in lows] + [(i + 1, i) for i in lows]


def local(kernel, inputs, shapes, scratch=(), megabytes=8, scalars=1):
    return pl.pallas_call(
        kernel,
        out_shape=[jax.ShapeDtypeStruct(shape, dtype) for shape, dtype in shapes],
        in_specs=[SMEM] * scalars + [VMEM] * (len(inputs) - scalars),
        out_specs=[VMEM] * len(shapes),
        scratch_shapes=[pltpu.VMEM(shape, jnp.float32) for shape in scratch],
        compiler_params=pltpu.CompilerParams(vmem_limit_bytes=megabytes << 20),
        name=kernel.__name__,
    )(*inputs)


def lanes_of(ref, x, width):
    return ref[:, x * width : (x + 1) * width]


def to_lanes(source_ref, held_ref, sems, wide_ref, out_ref, signs_ref=None):
    snaps, parts, depth, width = source_ref.shape
    pieces = sems.shape[0]
    step = snaps // pieces
    copies = [
        pltpu.make_async_copy(
            source_ref.at[i * step : (i + 1) * step], held_ref.at[i * step : (i + 1) * step], sems.at[i]
        )
        for i in range(pieces)
    ]
    for copy in copies:
        copy.start()
    tall = step * parts * depth
    for i, copy in enumerate(copies):
        copy.wait()
        values = held_ref[i * step : (i + 1) * step].astype(jnp.float32).reshape(tall, width)
        wide_ref[i * tall : (i + 1) * tall, :] = values
        for c in range(parts):
            for x in range(depth):
                piece = wide_ref[pl.ds(i * tall + c * depth + x, step, stride=parts * depth), :]
                if signs_ref is not None:
                    piece = piece * (2 * signs_ref[x : x + 1, :] - 1).astype(jnp.float32)
                low = c * snaps + i * step
                out_ref[low : low + step, x * width : (x + 1) * width] = piece.astype(out_ref.dtype)


def field_kernel(flags_ref, field_ref, lanes_ref, flat_ref, rim_a_ref, rim_b_ref, held_ref, wide_ref, sems):
    snaps, _, depth, width = field_ref.shape
    to_lanes(field_ref, held_ref, sems, wide_ref, lanes_ref)
    flat_ref[...] = lanes_ref[: 2 * snaps, :]
    odd = flags_ref[1] == 1
    first = lanes_ref[snaps:, :width].astype(jnp.float32)
    last = lanes_ref[snaps:, (depth - 1) * width :].astype(jnp.float32)
    rim_a_ref[...] = jnp.where(odd, first, last).astype(rim_a_ref.dtype)
    rim_b_ref[...] = jnp.where(odd, last, first).astype(rim_b_ref.dtype)


def velocity_kernel(
    flags_ref,
    velocity_ref,
    test_ref,
    signs_ref,
    pair_ref,
    matrix_ref,
    held_ref,
    wide_ref,
    sems,
    bits_ref,
    bits_sem,
    held_signs_ref,
    signs_sem,
):
    snaps, parts = velocity_ref.shape[:2]
    copy_signs = pltpu.make_async_copy(signs_ref, held_signs_ref, signs_sem)
    copy_signs.start()
    copy = pltpu.make_async_copy(test_ref, bits_ref, bits_sem)
    copy.start()
    copy_signs.wait()
    to_lanes(velocity_ref, held_ref, sems, wide_ref, pair_ref, held_signs_ref)
    copy.wait()
    columns = bits_ref.shape[0]
    width = wide_ref.shape[1]
    for low in range(0, bits_ref.shape[1], width):
        wide_ref[:columns, :] = (2 * bits_ref[:, low : low + width] - 1).astype(jnp.float32)
        for c in range(2 * parts):
            piece = wide_ref[pl.ds(c, snaps, stride=2 * parts), :]
            matrix_ref[c * snaps : (c + 1) * snaps, low : low + width] = piece.astype(matrix_ref.dtype)


def relay(kernel, flags, inputs, in_vmem, shapes, scratch=()):
    snaps, parts, depth, width = inputs[0].shape
    held = [pltpu.VMEM(inputs[0].shape, inputs[0].dtype), pltpu.VMEM((snaps * parts * depth, width), jnp.float32)]
    return pl.pallas_call(
        kernel,
        out_shape=[jax.ShapeDtypeStruct(shape, dtype) for shape, dtype in shapes],
        in_specs=[SMEM] + [pl.BlockSpec(memory_space=pl.ANY)] * len(inputs) + [VMEM] * len(in_vmem),
        out_specs=[VMEM] * len(shapes),
        scratch_shapes=held + [pltpu.SemaphoreType.DMA((4,))] + list(scratch),
        compiler_params=pltpu.CompilerParams(vmem_limit_bytes=8 << 20),
        name=kernel.__name__,
    )(flags, *[pltpu.with_memory_space_constraint(array, pltpu.HBM) for array in inputs], *in_vmem)


def curl_kernel(flags_ref, field_ref, plane_a_ref, plane_b_ref, rim_a_ref, rim_b_ref, signs_ref, current_ref):
    snaps = rim_a_ref.shape[0] // 2
    width = rim_a_ref.shape[1]
    depth = field_ref.shape[1] // width
    upward = 0.5 - flags_ref[0].astype(jnp.float32)
    odd_block = flags_ref[1] == 1
    lane = lax.broadcasted_iota(jnp.int32, (snaps, width), 1)

    def field(c, x):
        return lanes_of(field_ref.at[c * snaps : (c + 1) * snaps], x, width).astype(jnp.float32)

    def over_x(c, x):
        rim_a = rim_a_ref[(c - 1) * snaps : c * snaps, :].astype(jnp.float32)
        rim_b = rim_b_ref[(c - 1) * snaps : c * snaps, :].astype(jnp.float32)
        low = field(c, x - 1) if x else jnp.where(odd_block, rim_a, rim_b)
        high = field(c, x + 1) if x < depth - 1 else jnp.where(odd_block, rim_b, rim_a)
        return (high - low) * 0.5

    def over_y(c, x):
        values = field(c, x)
        low = jnp.where(lane == 0, 0.0, pltpu.roll(values, 1, 1))
        high = jnp.where(lane == width - 1, 0.0, pltpu.roll(values, width - 1, 1))
        return (high - low) * 0.5

    def over_z(c, x):
        a = lanes_of(plane_a_ref.at[c * snaps : (c + 1) * snaps], x, width).astype(jnp.float32)
        b = lanes_of(plane_b_ref.at[c * snaps : (c + 1) * snaps], x, width).astype(jnp.float32)
        return (a - b) * upward

    for x in range(depth):
        sign = (2 * signs_ref[x : x + 1, :] - 1).astype(jnp.float32)
        current = (
            over_y(2, x) - over_z(1, x),
            over_z(0, x) - over_x(2, x),
            over_x(1, x) - over_y(0, x),
        )
        for c, values in enumerate(current):
            current_ref[c * snaps : (c + 1) * snaps, x * width : (x + 1) * width] = (values * sign).astype(
                current_ref.dtype
            )


def parts_kernel(flags_ref, wanted_ref, pair_ref, other_ref, current_ref, other_current_ref, matrix_ref, *refs):
    part_refs, held_ref = refs[:-1], refs[-1]
    rows, points = current_ref.shape
    width = held_ref.shape[1]
    halves = matrix_ref.shape[1] // width
    own_sign = (1 - 2 * flags_ref[0]).astype(jnp.float32)

    def sketch(values_ref, matrix):
        return lax.dot_general(values_ref, matrix, (TN, ((), ())), preferred_element_type=jnp.float32)

    plain = matrix_ref[...]
    turned = (plain.astype(jnp.float32) * own_sign).astype(plain.dtype)
    total = sketch(pair_ref[-rows:, :], turned[:rows]) + sketch(other_ref[-rows:, :], plain[:rows])
    total = total + sketch(current_ref[...], turned[rows:]) + sketch(other_current_ref[...], plain[rows:])
    for half in range(halves):
        held_ref[pl.ds(half, points, stride=halves), :] = total[:, half * width : (half + 1) * width]
    samples = part_refs[0].shape[0] // halves
    batch = 16
    for slot, part_ref in enumerate(part_refs):
        for first in range(0, samples, batch):
            at = [pl.multiple_of(wanted_ref[slot * samples + first + i], halves) for i in range(batch)]
            values = [held_ref[pl.ds(start, halves), :] for start in at]
            for i in range(batch):
                part_ref[(first + i) * halves : (first + i + 1) * halves, :] = values[i]


def gram_kernel(signs_ref, *refs):
    parts, (picked_ref, packed_ref, held_ref) = refs[:-3], refs[-3:]
    total = signs_ref[0] * parts[0][...]
    for slot in range(1, len(parts)):
        total = total + signs_ref[slot] * parts[slot][...]
    held_ref[...] = total
    samples, wide = picked_ref.shape
    width = held_ref.shape[1]
    halves = wide // width
    picked = [held_ref[pl.ds(half, samples, stride=halves), :] for half in range(halves)]
    picked = jnp.concatenate(picked, axis=1)
    picked_ref[...] = picked
    pack(product(picked.T, picked, NN) * signs_ref[len(parts)], packed_ref)


def product(a, b, dims):
    return lax.dot_general(
        a, b, (dims, ((), ())), precision=lax.Precision.HIGHEST, preferred_element_type=jnp.float32
    )


def in_three(x):
    high = x.astype(jnp.bfloat16)
    left = x - high.astype(jnp.float32)
    middle = left.astype(jnp.bfloat16)
    return high, middle, (left - middle.astype(jnp.float32)).astype(jnp.bfloat16)


def outer(a, b):
    (a0, a1, a2), (b0, b1, b2) = in_three(a), in_three(b)
    left = jnp.concatenate([a0, a0, a1, a0, a2, a1])
    right = jnp.concatenate([b0, b1, b0, b2, b0, b1])
    return lax.dot_general(left, right, (TN, ((), ())), preferred_element_type=jnp.float32)


def eliminate(a_ref, z_ref):
    n = a_ref.shape[0]
    blocks = n // ROWS
    row = lax.broadcasted_iota(jnp.int32, (ROWS, n), 0)
    lane = lax.broadcasted_iota(jnp.int32, (ROWS, n), 1)

    def spread(x):
        return jnp.broadcast_to(x, (ROWS, n))

    def column(block, c):
        return spread(block[:, c : c + 1])

    def line(block, k):
        return spread(block[k : k + 1, :])

    rest = [a_ref[b * ROWS : (b + 1) * ROWS, :] for b in range(blocks)]
    rest_z = [jnp.where(lane == row + b * ROWS, 1.0, 0.0) for b in range(blocks)]
    columns = [column(rest[0], c) for c in range(ROWS)]
    for b in range(blocks):
        start = b * ROWS
        pivots = {(k, c): line(columns[c], k) for c in range(ROWS) for k in range(c + 1)}
        top = [line(rest[b], k) for k in range(ROWS)]
        top_z = [line(rest_z[b], k) for k in range(ROWS)]
        following = range(b + 1, min(b + 2, blocks))
        for g in following:
            next_old = [column(rest[g], start + c) for c in range(ROWS)]
            columns = [column(rest[g], start + ROWS + c) for c in range(ROWS)]
        inverse = []
        for k in range(ROWS):
            inverse.append(1.0 / pivots[k, k])
            for i in range(k + 1, ROWS):
                times = pivots[k, i] * inverse[k]
                for c in range(i, ROWS):
                    pivots[i, c] = pivots[i, c] - times * pivots[k, c]
                top[i] = top[i] - times * top[k]
                top_z[i] = top_z[i] - times * top_z[k]
            for g in following:
                times = next_old[k] * inverse[k]
                columns = [values - times * line(next_old[k], c) for c, values in enumerate(columns)]
                for c in range(k + 1, ROWS):
                    next_old[c] = next_old[c] - times * pivots[k, c]
                rest[g] = rest[g] - times * top[k]
                rest_z[g] = rest_z[g] - times * top_z[k]
        for g in range(b + 2, min(b + NEAR, blocks)):
            old = [column(rest[g], start + c) for c in range(ROWS)]
            for k in range(ROWS):
                times = old[k] * inverse[k]
                for c in range(k + 1, ROWS):
                    old[c] = old[c] - times * pivots[k, c]
                rest[g] = rest[g] - times * top[k]
                rest_z[g] = rest_z[g] - times * top_z[k]
        done, done_z = jnp.zeros((ROWS, n), jnp.float32), jnp.zeros((ROWS, n), jnp.float32)
        for k in range(ROWS):
            scale = lax.rsqrt(pivots[k, k])
            done = jnp.where(row == k, top[k] * scale, done)
            done_z = jnp.where(row == k, top_z[k] * scale, done_z)
        done = jnp.where(lane >= row + start, done, 0.0)
        a_ref[start : start + ROWS, :] = done
        z_ref[start : start + ROWS, :] = done_z
        far = (b + NEAR) * ROWS
        if far < n:
            update = outer(done[:, far:], jnp.concatenate([done, done_z], axis=1))
            for g in range(b + NEAR, blocks):
                low = g * ROWS - far
                rest[g] = rest[g] - update[low : low + ROWS, :n]
                rest_z[g] = rest_z[g] - update[low : low + ROWS, n:]


def pack(gram, packed_ref):
    n = gram.shape[0]
    q, h = n // 4, n // 2
    lane = lax.broadcasted_iota(jnp.int32, (q, h), 1)
    packed_ref[:q, :] = gram[:q, :]
    packed_ref[q:h, :h] = jnp.where(lane < q, gram[h : h + q, h:], gram[q:h, :h])
    packed_ref[q:h, h:] = gram[q:h, h:]
    packed_ref[h:, :h] = gram[h + q : h + q + q // 2, h:]
    packed_ref[h:, h:] = gram[h + q + q // 2 :, h:]


def unpack(packed):
    n = packed.shape[1]
    q, h = n // 4, n // 2
    row = lax.broadcasted_iota(jnp.int32, (h, h), 0)
    lane = lax.broadcasted_iota(jnp.int32, (h, h), 1)
    top = packed[:h, :h]
    first = jnp.where((row >= q) & (lane < q), top.T, top)
    bottom = jnp.concatenate([packed[q:h, :h], packed[h:, :h], packed[h:, h:]])
    last = jnp.where((row < q) & (lane >= q), bottom.T, bottom)
    return first, packed[:h, h:], last


def parity_sign(a, b):
    both = jnp.bitwise_and(a, b)
    return 1.0 - 2.0 * (lax.population_count(both) % 2).astype(jnp.float32)


def doubled(rows, bit):
    return jnp.concatenate([rows, lax.ppermute(rows, "mix", xor_route(lax.axis_size("mix"), bit))])


def sampled_mixing(flags, pair, other, current, matrix, wanted):
    planes = lax.axis_size("mix")
    mine = lax.axis_index("mix")
    targets, samples = wanted.shape
    halves = matrix.shape[1] // LANES
    part = ((samples * halves, LANES), jnp.float32)
    other_current = lax.ppermute(current, "mix", xor_route(planes, 1))
    inputs = (flags, wanted.reshape(-1) * halves, pair, other, current, other_current, matrix)
    scratch = ((current.shape[1] * halves, LANES),)
    parts = local(parts_kernel, inputs, [part] * targets, scratch, megabytes=12, scalars=2)
    hops = range(2, planes, 2)
    arrived = [parts[0]] + [lax.ppermute(part, "mix", xor_route(planes, k)) for part, k in zip(parts[1:], hops)]
    return arrived, [parity_sign(mine, (mine ^ k) - mine % 2) for k in range(0, planes, 2)]


def whole_mixing(pair, current, matrix, wanted):
    planes = lax.axis_size("mix")
    mine = lax.axis_index("mix")
    snapshot = jnp.concatenate([pair[-current.shape[0] :], current])
    values = lax.dot_general(snapshot, matrix, (((0,), (0,)), ((), ())), preferred_element_type=jnp.float32)
    for level in range(planes.bit_length() - 1):
        partner = lax.ppermute(values, "mix", xor_route(planes, 1 << level))
        upper_bit = mine // (1 << level) % 2
        values = jnp.where(upper_bit == 1, partner - values, values + partner)
    return [jnp.take(values, wanted[0], axis=0).reshape(-1, LANES)], [jnp.float32(1.0)]


def sum_over_mesh(packed):
    planes, blocks = lax.axis_size("mix"), lax.axis_size("row")
    half_rows = packed.shape[0] // 2
    low, high = packed[:half_rows], packed[half_rows:]
    if planes > 8 or blocks != 4:
        low, high = lax.psum((low, high), MESH_AXES)
        return low, high, jnp.int32(0)
    core = lax.axis_index("mix") % 2
    half = jnp.where(core == 0, low, high)
    half = half + lax.ppermute(jnp.where(core == 0, high, low), "mix", xor_route(planes, 1))
    half = half + sum(lax.ppermute(half, "mix", xor_route(planes, k)) for k in range(2, planes, 2))
    half = half + sum(lax.ppermute(half, "row", xor_route(blocks, k)) for k in range(blocks - 1, 0, -1))
    return half, lax.ppermute(half, "mix", xor_route(planes, 1)), core


def finish_kernel(core_ref, half_ref, other_ref, picked_ref, basis_ref, factor_ref, a_ref, first_ref, second_ref):
    side = a_ref.shape[0]
    half, other = half_ref[...], other_ref[...]
    swap = core_ref[0] != 0
    packed = jnp.concatenate([jnp.where(swap, other, half), jnp.where(swap, half, other)])
    corner, right, last = unpack(packed)
    a_ref[...] = corner
    eliminate(a_ref, first_ref)
    first = first_ref[...]
    across = product(first, right, NN)
    down = product(right.T, first, NT)
    factor_ref[:side, :side] = a_ref[...]
    factor_ref[:side, side:] = across
    factor_ref[side:, :side] = jnp.zeros_like(across)
    a_ref[...] = last - product(down, across, NN)
    solved = product(picked_ref[:, :side], first, NT)
    basis_ref[:, :side] = solved
    left_over = picked_ref[:, side:] - product(solved, across, NN)
    eliminate(a_ref, second_ref)
    basis_ref[:, side:] = product(left_over, second_ref[...], NT)
    factor_ref[side:, side:] = a_ref[...]


def finish(half, other, core, picked):
    n = picked.shape[1]
    shapes = [(picked.shape, jnp.float32), ((n, n), jnp.float32)]
    scratch = ((n // 2, n // 2),) * 3
    return local(finish_kernel, (core.reshape(1), half, other, picked), shapes, scratch)


def on_device(velocity, field_b, test_signs, row_signs, sample_index):
    snaps, parts, _, depth, width = field_b.shape
    sketch_width = test_signs.shape[1]
    planes, blocks = lax.axis_size("mix"), lax.axis_size("row")
    samples = sample_index.shape[-1]
    points = depth * width
    flags = jnp.stack([lax.axis_index("mix") % 2, lax.axis_index("row") % 2]).astype(jnp.int32)
    signs = row_signs[0]
    lanes = ((parts * snaps, points), jnp.bfloat16)
    flat = ((2 * snaps, points), jnp.bfloat16)
    rim = ((2 * snaps, width), jnp.bfloat16)
    sampled_bytes = (planes // 2 - 1) * samples * sketch_width
    whole_bytes = (planes.bit_length() - 1) * points * sketch_width
    sampled = sampled_bytes < whole_bytes
    wanted = sample_index.reshape(1, -1)
    if sampled:
        wanted = doubled(wanted, 2)
    field, flat, rim_a, rim_b = relay(field_kernel, flags, [field_b[:, :, 0]], [], [lanes, flat, rim, rim])
    plane_b = lax.ppermute(flat, "mix", pair_route(planes, 1))
    rim_a = lax.ppermute(rim_a, "row", pair_route(blocks, 0))
    rim_b = lax.ppermute(rim_b, "row", pair_route(blocks, 1))
    matrix = ((2 * parts * snaps, sketch_width), jnp.bfloat16)
    scratch = [pltpu.VMEM(test_signs.shape, jnp.int32), pltpu.SemaphoreType.DMA]
    scratch += [pltpu.VMEM(signs.shape, jnp.int32), pltpu.SemaphoreType.DMA]
    inputs = [velocity[:, :, 0], test_signs, signs]
    pair, matrix = relay(velocity_kernel, flags, inputs, [], [lanes, matrix], scratch)
    plane_a = lax.ppermute(flat, "mix", pair_route(planes, 0))
    pair, wanted = lax.optimization_barrier((pair, wanted))
    other = lax.ppermute(pair, "mix", pair_route(planes, 0))
    if sampled:
        for level in range(2, planes.bit_length() - 1):
            wanted = doubled(wanted, 1 << level)
    (current,) = local(curl_kernel, (flags, field, plane_a, plane_b, rim_a, rim_b, signs), [lanes])
    if sampled:
        added, part_signs = sampled_mixing(flags, pair, other, current, matrix, wanted)
    else:
        added, part_signs = whole_mixing(pair, current, matrix, wanted)
    scale = 1.0 / math.sqrt(6 * snaps * planes)
    factors = jnp.stack([sign * scale for sign in part_signs] + [jnp.float32(1.0 / (planes * blocks * samples))])
    picked, packed = local(
        gram_kernel,
        (factors, *added),
        [((samples, sketch_width), jnp.float32), ((sketch_width * 5 // 8, sketch_width), jnp.float32)],
        (added[0].shape,),
    )
    basis_rows, factor = finish(*sum_over_mesh(packed), picked)
    return basis_rows.reshape(sample_index.shape + (sketch_width,)), factor


def solution(mesh):
    return jax.shard_map(
        on_device,
        mesh=mesh,
        in_specs=(
            P(None, None, "mix", "row", None),
            P(None, None, "mix", "row", None),
            P(),
            P("mix", "row", None),
            P("mix", "row", None),
        ),
        out_specs=(P("mix", "row", None, None), P()),
        check_vma=False,
    )
```

```python
import math

import jax
import jax.numpy as jnp
from jax import lax
from jax.experimental import pallas as pl
from jax.experimental.pallas import tpu as pltpu
from jax.sharding import PartitionSpec as P

MESH_AXES = ("row", "mix")
ROWS = 8
LANES = 128
NEAR = 4
NN, NT, TN = ((1,), (0,)), ((1,), (1,)), ((0,), (0,))
SMEM = pl.BlockSpec(memory_space=pltpu.SMEM)
VMEM = pl.BlockSpec(memory_space=pltpu.VMEM)


def xor_route(count, bits):
    return [(i, i ^ bits) for i in range(count) if i ^ bits < count]


def pair_route(count, first):
    lows = range(first, count - 1, 2)
    return [(i, i + 1) for i in lows] + [(i + 1, i) for i in lows]


def local(kernel, inputs, shapes, scratch=(), megabytes=8, scalars=1):
    return pl.pallas_call(
        kernel,
        out_shape=[jax.ShapeDtypeStruct(shape, dtype) for shape, dtype in shapes],
        in_specs=[SMEM] * scalars + [VMEM] * (len(inputs) - scalars),
        out_specs=[VMEM] * len(shapes),
        scratch_shapes=[pltpu.VMEM(shape, jnp.float32) for shape in scratch],
        compiler_params=pltpu.CompilerParams(vmem_limit_bytes=megabytes << 20),
        name=kernel.__name__,
    )(*inputs)


def lanes_of(ref, x, width):
    return ref[:, x * width : (x + 1) * width]


def to_lanes(source_ref, held_ref, sems, wide_ref, out_ref, signs_ref=None, first=()):
    snaps, parts, depth, width = source_ref.shape
    pieces = sems.shape[0]
    step = snaps // pieces
    copies = [
        pltpu.make_async_copy(
            source_ref.at[i * step : (i + 1) * step], held_ref.at[i * step : (i + 1) * step], sems.at[i]
        )
        for i in range(pieces)
    ]
    for copy in [*first, *copies]:
        copy.start()
    for copy in first:
        copy.wait()
    tall = step * parts * depth
    for i, copy in enumerate(copies):
        copy.wait()
        values = held_ref[i * step : (i + 1) * step].astype(jnp.float32).reshape(tall, width)
        wide_ref[i * tall : (i + 1) * tall, :] = values
        for c in range(parts):
            for x in range(depth):
                piece = wide_ref[pl.ds(i * tall + c * depth + x, step, stride=parts * depth), :]
                if signs_ref is not None:
                    piece = piece * (2 * signs_ref[x : x + 1, :] - 1).astype(jnp.float32)
                low = c * snaps + i * step
                out_ref[low : low + step, x * width : (x + 1) * width] = piece.astype(out_ref.dtype)


def field_kernel(flags_ref, field_ref, lanes_ref, flat_ref, rim_a_ref, rim_b_ref, held_ref, wide_ref, sems):
    snaps, _, depth, width = field_ref.shape
    to_lanes(field_ref, held_ref, sems, wide_ref, lanes_ref)
    flat_ref[...] = lanes_ref[: 2 * snaps, :]
    odd = flags_ref[1] == 1
    first = lanes_ref[snaps:, :width].astype(jnp.float32)
    last = lanes_ref[snaps:, (depth - 1) * width :].astype(jnp.float32)
    rim_a_ref[...] = jnp.where(odd, first, last).astype(rim_a_ref.dtype)
    rim_b_ref[...] = jnp.where(odd, last, first).astype(rim_b_ref.dtype)


def velocity_kernel(
    flags_ref,
    velocity_ref,
    test_ref,
    signs_ref,
    pair_ref,
    matrix_ref,
    held_ref,
    wide_ref,
    sems,
    bits_ref,
    bits_sem,
    held_signs_ref,
    signs_sem,
):
    snaps, parts = velocity_ref.shape[:2]
    copy_signs = pltpu.make_async_copy(signs_ref, held_signs_ref, signs_sem)
    copy = pltpu.make_async_copy(test_ref, bits_ref, bits_sem)
    copy.start()
    to_lanes(velocity_ref, held_ref, sems, wide_ref, pair_ref, held_signs_ref, [copy_signs])
    copy.wait()
    columns = bits_ref.shape[0]
    width = wide_ref.shape[1]
    for low in range(0, bits_ref.shape[1], width):
        wide_ref[:columns, :] = (2 * bits_ref[:, low : low + width] - 1).astype(jnp.float32)
        for c in range(2 * parts):
            piece = wide_ref[pl.ds(c, snaps, stride=2 * parts), :]
            matrix_ref[c * snaps : (c + 1) * snaps, low : low + width] = piece.astype(matrix_ref.dtype)


def relay(kernel, flags, inputs, in_vmem, shapes, scratch=()):
    snaps, parts, depth, width = inputs[0].shape
    held = [pltpu.VMEM(inputs[0].shape, inputs[0].dtype), pltpu.VMEM((snaps * parts * depth, width), jnp.float32)]
    return pl.pallas_call(
        kernel,
        out_shape=[jax.ShapeDtypeStruct(shape, dtype) for shape, dtype in shapes],
        in_specs=[SMEM] + [pl.BlockSpec(memory_space=pl.ANY)] * len(inputs) + [VMEM] * len(in_vmem),
        out_specs=[VMEM] * len(shapes),
        scratch_shapes=held + [pltpu.SemaphoreType.DMA((4,))] + list(scratch),
        compiler_params=pltpu.CompilerParams(vmem_limit_bytes=8 << 20),
        name=kernel.__name__,
    )(flags, *[pltpu.with_memory_space_constraint(array, pltpu.HBM) for array in inputs], *in_vmem)


def curl_kernel(flags_ref, field_ref, plane_a_ref, plane_b_ref, rim_a_ref, rim_b_ref, signs_ref, current_ref):
    snaps = rim_a_ref.shape[0] // 2
    width = rim_a_ref.shape[1]
    depth = field_ref.shape[1] // width
    upward = 0.5 - flags_ref[0].astype(jnp.float32)
    odd_block = flags_ref[1] == 1
    lane = lax.broadcasted_iota(jnp.int32, (snaps, width), 1)

    def field(c, x):
        return lanes_of(field_ref.at[c * snaps : (c + 1) * snaps], x, width).astype(jnp.float32)

    def over_x(c, x):
        rim_a = rim_a_ref[(c - 1) * snaps : c * snaps, :].astype(jnp.float32)
        rim_b = rim_b_ref[(c - 1) * snaps : c * snaps, :].astype(jnp.float32)
        low = field(c, x - 1) if x else jnp.where(odd_block, rim_a, rim_b)
        high = field(c, x + 1) if x < depth - 1 else jnp.where(odd_block, rim_b, rim_a)
        return (high - low) * 0.5

    def over_y(c, x):
        values = field(c, x)
        low = jnp.where(lane == 0, 0.0, pltpu.roll(values, 1, 1))
        high = jnp.where(lane == width - 1, 0.0, pltpu.roll(values, width - 1, 1))
        return (high - low) * 0.5

    def over_z(c, x):
        a = lanes_of(plane_a_ref.at[c * snaps : (c + 1) * snaps], x, width).astype(jnp.float32)
        b = lanes_of(plane_b_ref.at[c * snaps : (c + 1) * snaps], x, width).astype(jnp.float32)
        return (a - b) * upward

    for x in range(depth):
        sign = (2 * signs_ref[x : x + 1, :] - 1).astype(jnp.float32)
        current = (
            over_y(2, x) - over_z(1, x),
            over_z(0, x) - over_x(2, x),
            over_x(1, x) - over_y(0, x),
        )
        for c, values in enumerate(current):
            current_ref[c * snaps : (c + 1) * snaps, x * width : (x + 1) * width] = (values * sign).astype(
                current_ref.dtype
            )


def parts_kernel(flags_ref, wanted_ref, pair_ref, other_ref, current_ref, other_current_ref, matrix_ref, *refs):
    part_refs, held_ref = refs[:-1], refs[-1]
    rows, points = current_ref.shape
    width = held_ref.shape[1]
    halves = matrix_ref.shape[1] // width
    own_sign = (1 - 2 * flags_ref[0]).astype(jnp.float32)

    def sketch(values_ref, matrix):
        return lax.dot_general(values_ref, matrix, (TN, ((), ())), preferred_element_type=jnp.float32)

    plain = matrix_ref[...]
    turned = (plain.astype(jnp.float32) * own_sign).astype(plain.dtype)
    total = sketch(pair_ref[-rows:, :], turned[:rows]) + sketch(other_ref[-rows:, :], plain[:rows])
    total = total + sketch(current_ref[...], turned[rows:]) + sketch(other_current_ref[...], plain[rows:])
    for half in range(halves):
        held_ref[pl.ds(half, points, stride=halves), :] = total[:, half * width : (half + 1) * width]
    samples = part_refs[0].shape[0] // halves
    batch = 16
    for slot, part_ref in enumerate(part_refs):
        for first in range(0, samples, batch):
            at = [pl.multiple_of(wanted_ref[slot * samples + first + i], halves) for i in range(batch)]
            values = [held_ref[pl.ds(start, halves), :] for start in at]
            for i in range(batch):
                part_ref[(first + i) * halves : (first + i + 1) * halves, :] = values[i]


def gram_kernel(signs_ref, *refs):
    parts, (picked_ref, packed_ref, held_ref) = refs[:-3], refs[-3:]
    total = signs_ref[0] * parts[0][...]
    for slot in range(1, len(parts)):
        total = total + signs_ref[slot] * parts[slot][...]
    held_ref[...] = total
    samples, wide = picked_ref.shape
    width = held_ref.shape[1]
    halves = wide // width
    picked = [held_ref[pl.ds(half, samples, stride=halves), :] for half in range(halves)]
    picked = jnp.concatenate(picked, axis=1)
    picked_ref[...] = picked
    pack(product(picked.T, picked, NN) * signs_ref[len(parts)], packed_ref)


def product(a, b, dims):
    return lax.dot_general(
        a, b, (dims, ((), ())), precision=lax.Precision.HIGHEST, preferred_element_type=jnp.float32
    )


def in_three(x):
    high = x.astype(jnp.bfloat16)
    left = x - high.astype(jnp.float32)
    middle = left.astype(jnp.bfloat16)
    return high, middle, (left - middle.astype(jnp.float32)).astype(jnp.bfloat16)


def outer(a, b):
    (a0, a1, a2), (b0, b1, b2) = in_three(a), in_three(b)
    left = jnp.concatenate([a0, a0, a1, a0, a2, a1])
    right = jnp.concatenate([b0, b1, b0, b2, b0, b1])
    return lax.dot_general(left, right, (TN, ((), ())), preferred_element_type=jnp.float32)


def eliminate(a_ref, z_ref):
    n = a_ref.shape[0]
    blocks = n // ROWS
    row = lax.broadcasted_iota(jnp.int32, (ROWS, n), 0)
    lane = lax.broadcasted_iota(jnp.int32, (ROWS, n), 1)

    def spread(x):
        return jnp.broadcast_to(x, (ROWS, n))

    def column(block, c):
        return spread(block[:, c : c + 1])

    def line(block, k):
        return spread(block[k : k + 1, :])

    rest = [a_ref[b * ROWS : (b + 1) * ROWS, :] for b in range(blocks)]
    rest_z = [jnp.where(lane == row + b * ROWS, 1.0, 0.0) for b in range(blocks)]
    columns = [column(rest[0], c) for c in range(ROWS)]
    for b in range(blocks):
        start = b * ROWS
        pivots = {(k, c): line(columns[c], k) for c in range(ROWS) for k in range(c + 1)}
        top = [line(rest[b], k) for k in range(ROWS)]
        top_z = [line(rest_z[b], k) for k in range(ROWS)]
        following = range(b + 1, min(b + 2, blocks))
        for g in following:
            next_old = [column(rest[g], start + c) for c in range(ROWS)]
            columns = [column(rest[g], start + ROWS + c) for c in range(ROWS)]
        inverse = []
        for k in range(ROWS):
            inverse.append(1.0 / pivots[k, k])
            for i in range(k + 1, ROWS):
                times = pivots[k, i] * inverse[k]
                for c in range(i, ROWS):
                    pivots[i, c] = pivots[i, c] - times * pivots[k, c]
                top[i] = top[i] - times * top[k]
                top_z[i] = top_z[i] - times * top_z[k]
            for g in following:
                times = next_old[k] * inverse[k]
                columns = [values - times * line(next_old[k], c) for c, values in enumerate(columns)]
                for c in range(k + 1, ROWS):
                    next_old[c] = next_old[c] - times * pivots[k, c]
                rest[g] = rest[g] - times * top[k]
                rest_z[g] = rest_z[g] - times * top_z[k]
        for g in range(b + 2, min(b + NEAR, blocks)):
            old = [column(rest[g], start + c) for c in range(ROWS)]
            for k in range(ROWS):
                times = old[k] * inverse[k]
                for c in range(k + 1, ROWS):
                    old[c] = old[c] - times * pivots[k, c]
                rest[g] = rest[g] - times * top[k]
                rest_z[g] = rest_z[g] - times * top_z[k]
        done, done_z = jnp.zeros((ROWS, n), jnp.float32), jnp.zeros((ROWS, n), jnp.float32)
        for k in range(ROWS):
            scale = lax.rsqrt(pivots[k, k])
            done = jnp.where(row == k, top[k] * scale, done)
            done_z = jnp.where(row == k, top_z[k] * scale, done_z)
        done = jnp.where(lane >= row + start, done, 0.0)
        a_ref[start : start + ROWS, :] = done
        z_ref[start : start + ROWS, :] = done_z
        far = (b + NEAR) * ROWS
        if far < n:
            update = outer(done[:, far:], jnp.concatenate([done, done_z], axis=1))
            for g in range(b + NEAR, blocks):
                low = g * ROWS - far
                rest[g] = rest[g] - update[low : low + ROWS, :n]
                rest_z[g] = rest_z[g] - update[low : low + ROWS, n:]


def pack(gram, packed_ref):
    n = gram.shape[0]
    q, h = n // 4, n // 2
    lane = lax.broadcasted_iota(jnp.int32, (q, h), 1)
    packed_ref[:q, :] = gram[:q, :]
    packed_ref[q:h, :h] = jnp.where(lane < q, gram[h : h + q, h:], gram[q:h, :h])
    packed_ref[q:h, h:] = gram[q:h, h:]
    packed_ref[h:, :h] = gram[h + q : h + q + q // 2, h:]
    packed_ref[h:, h:] = gram[h + q + q // 2 :, h:]


def unpack(packed):
    n = packed.shape[1]
    q, h = n // 4, n // 2
    row = lax.broadcasted_iota(jnp.int32, (h, h), 0)
    lane = lax.broadcasted_iota(jnp.int32, (h, h), 1)
    top = packed[:h, :h]
    first = jnp.where((row >= q) & (lane < q), top.T, top)
    bottom = jnp.concatenate([packed[q:h, :h], packed[h:, :h], packed[h:, h:]])
    last = jnp.where((row < q) & (lane >= q), bottom.T, bottom)
    return first, packed[:h, h:], last


def parity_sign(a, b):
    both = jnp.bitwise_and(a, b)
    return 1.0 - 2.0 * (lax.population_count(both) % 2).astype(jnp.float32)


def doubled(rows, bit):
    return jnp.concatenate([rows, lax.ppermute(rows, "mix", xor_route(lax.axis_size("mix"), bit))])


def sampled_mixing(flags, pair, other, current, matrix, wanted):
    planes = lax.axis_size("mix")
    mine = lax.axis_index("mix")
    targets, samples = wanted.shape
    halves = matrix.shape[1] // LANES
    part = ((samples * halves, LANES), jnp.float32)
    other_current = lax.ppermute(current, "mix", xor_route(planes, 1))
    inputs = (flags, wanted.reshape(-1) * halves, pair, other, current, other_current, matrix)
    scratch = ((current.shape[1] * halves, LANES),)
    parts = local(parts_kernel, inputs, [part] * targets, scratch, megabytes=12, scalars=2)
    hops = [0]
    for level in range(planes.bit_length() - 2, 0, -1):
        hops += [hop ^ 1 << level for hop in hops]
    arrived = [parts[0]] + [lax.ppermute(part, "mix", xor_route(planes, k)) for part, k in zip(parts[1:], hops[1:])]
    return arrived, [parity_sign(mine, (mine ^ k) - mine % 2) for k in hops]


def whole_mixing(pair, current, matrix, wanted):
    planes = lax.axis_size("mix")
    mine = lax.axis_index("mix")
    snapshot = jnp.concatenate([pair[-current.shape[0] :], current])
    values = lax.dot_general(snapshot, matrix, (((0,), (0,)), ((), ())), preferred_element_type=jnp.float32)
    for level in range(planes.bit_length() - 1):
        partner = lax.ppermute(values, "mix", xor_route(planes, 1 << level))
        upper_bit = mine // (1 << level) % 2
        values = jnp.where(upper_bit == 1, partner - values, values + partner)
    return [jnp.take(values, wanted[0], axis=0).reshape(-1, LANES)], [jnp.float32(1.0)]


def sum_over_mesh(packed):
    planes, blocks = lax.axis_size("mix"), lax.axis_size("row")
    half_rows = packed.shape[0] // 2
    low, high = packed[:half_rows], packed[half_rows:]
    if planes > 8 or blocks != 4:
        low, high = lax.psum((low, high), MESH_AXES)
        return low, high, jnp.int32(0)
    core = lax.axis_index("mix") % 2
    half = jnp.where(core == 0, low, high)
    half = half + lax.ppermute(jnp.where(core == 0, high, low), "mix", xor_route(planes, 1))
    half = half + sum(lax.ppermute(half, "mix", xor_route(planes, k)) for k in range(2, planes, 2))
    half = half + sum(lax.ppermute(half, "row", xor_route(blocks, k)) for k in range(blocks - 1, 0, -1))
    return half, lax.ppermute(half, "mix", xor_route(planes, 1)), core


def finish_kernel(core_ref, half_ref, other_ref, picked_ref, basis_ref, factor_ref, a_ref, first_ref, second_ref):
    side = a_ref.shape[0]
    half, other = half_ref[...], other_ref[...]
    swap = core_ref[0] != 0
    packed = jnp.concatenate([jnp.where(swap, other, half), jnp.where(swap, half, other)])
    corner, right, last = unpack(packed)
    a_ref[...] = corner
    eliminate(a_ref, first_ref)
    first = first_ref[...]
    across = product(first, right, NN)
    down = product(right.T, first, NT)
    factor_ref[:side, :side] = a_ref[...]
    factor_ref[:side, side:] = across
    factor_ref[side:, :side] = jnp.zeros_like(across)
    a_ref[...] = last - product(down, across, NN)
    solved = product(picked_ref[:, :side], first, NT)
    basis_ref[:, :side] = solved
    left_over = picked_ref[:, side:] - product(solved, across, NN)
    eliminate(a_ref, second_ref)
    basis_ref[:, side:] = product(left_over, second_ref[...], NT)
    factor_ref[side:, side:] = a_ref[...]


def finish(half, other, core, picked):
    n = picked.shape[1]
    shapes = [(picked.shape, jnp.float32), ((n, n), jnp.float32)]
    scratch = ((n // 2, n // 2),) * 3
    return local(finish_kernel, (core.reshape(1), half, other, picked), shapes, scratch)


def on_device(velocity, field_b, test_signs, row_signs, sample_index):
    snaps, parts, _, depth, width = field_b.shape
    sketch_width = test_signs.shape[1]
    planes, blocks = lax.axis_size("mix"), lax.axis_size("row")
    samples = sample_index.shape[-1]
    points = depth * width
    flags = jnp.stack([lax.axis_index("mix") % 2, lax.axis_index("row") % 2]).astype(jnp.int32)
    signs = row_signs[0]
    lanes = ((parts * snaps, points), jnp.bfloat16)
    flat = ((2 * snaps, points), jnp.bfloat16)
    rim = ((2 * snaps, width), jnp.bfloat16)
    sampled_bytes = (planes // 2 - 1) * samples * sketch_width
    whole_bytes = (planes.bit_length() - 1) * points * sketch_width
    sampled = sampled_bytes < whole_bytes
    wanted = sample_index.reshape(1, -1)
    if sampled:
        wanted = doubled(wanted, planes // 2)
    field, flat, rim_a, rim_b = relay(field_kernel, flags, [field_b[:, :, 0]], [], [lanes, flat, rim, rim])
    plane_b = lax.ppermute(flat, "mix", pair_route(planes, 1))
    rim_a = lax.ppermute(rim_a, "row", pair_route(blocks, 0))
    rim_b = lax.ppermute(rim_b, "row", pair_route(blocks, 1))
    matrix = ((2 * parts * snaps, sketch_width), jnp.bfloat16)
    scratch = [pltpu.VMEM(test_signs.shape, jnp.int32), pltpu.SemaphoreType.DMA]
    scratch += [pltpu.VMEM(signs.shape, jnp.int32), pltpu.SemaphoreType.DMA]
    inputs = [velocity[:, :, 0], test_signs, signs]
    pair, matrix = relay(velocity_kernel, flags, inputs, [], [lanes, matrix], scratch)
    plane_a = lax.ppermute(flat, "mix", pair_route(planes, 0))
    pair, wanted = lax.optimization_barrier((pair, wanted))
    other = lax.ppermute(pair, "mix", pair_route(planes, 0))
    if sampled:
        for level in range(planes.bit_length() - 3, 0, -1):
            wanted = doubled(wanted, 1 << level)
    (current,) = local(curl_kernel, (flags, field, plane_a, plane_b, rim_a, rim_b, signs), [lanes])
    if sampled:
        added, part_signs = sampled_mixing(flags, pair, other, current, matrix, wanted)
    else:
        added, part_signs = whole_mixing(pair, current, matrix, wanted)
    scale = 1.0 / math.sqrt(6 * snaps * planes)
    factors = jnp.stack([sign * scale for sign in part_signs] + [jnp.float32(1.0 / (planes * blocks * samples))])
    picked, packed = local(
        gram_kernel,
        (factors, *added),
        [((samples, sketch_width), jnp.float32), ((sketch_width * 5 // 8, sketch_width), jnp.float32)],
        (added[0].shape,),
    )
    basis_rows, factor = finish(*sum_over_mesh(packed), picked)
    return basis_rows.reshape(sample_index.shape + (sketch_width,)), factor


def solution(mesh):
    return jax.shard_map(
        on_device,
        mesh=mesh,
        in_specs=(
            P(None, None, "mix", "row", None),
            P(None, None, "mix", "row", None),
            P(),
            P("mix", "row", None),
            P("mix", "row", None),
        ),
        out_specs=(P("mix", "row", None, None), P()),
        check_vma=False,
    )
```

```python
import math

import jax
import jax.numpy as jnp
from jax import lax
from jax.experimental import pallas as pl
from jax.experimental.pallas import tpu as pltpu
from jax.sharding import PartitionSpec as P

MESH_AXES = ("row", "mix")
ROWS = 8
LANES = 128
NEAR = 5
NN, NT, TN = ((1,), (0,)), ((1,), (1,)), ((0,), (0,))
SMEM = pl.BlockSpec(memory_space=pltpu.SMEM)
VMEM = pl.BlockSpec(memory_space=pltpu.VMEM)


def xor_route(count, bits):
    return [(i, i ^ bits) for i in range(count) if i ^ bits < count]


def pair_route(count, first):
    lows = range(first, count - 1, 2)
    return [(i, i + 1) for i in lows] + [(i + 1, i) for i in lows]


def local(kernel, inputs, shapes, scratch=(), megabytes=8, scalars=1):
    return pl.pallas_call(
        kernel,
        out_shape=[jax.ShapeDtypeStruct(shape, dtype) for shape, dtype in shapes],
        in_specs=[SMEM] * scalars + [VMEM] * (len(inputs) - scalars),
        out_specs=[VMEM] * len(shapes),
        scratch_shapes=[pltpu.VMEM(shape, jnp.float32) for shape in scratch],
        compiler_params=pltpu.CompilerParams(vmem_limit_bytes=megabytes << 20),
        name=kernel.__name__,
    )(*inputs)


def lanes_of(ref, x, width):
    return ref[:, x * width : (x + 1) * width]


def to_lanes(source_ref, held_ref, sems, wide_ref, out_ref, signs_ref=None, first=()):
    snaps, parts, depth, width = source_ref.shape
    pieces = sems.shape[0]
    step = snaps // pieces
    copies = [
        pltpu.make_async_copy(
            source_ref.at[i * step : (i + 1) * step], held_ref.at[i * step : (i + 1) * step], sems.at[i]
        )
        for i in range(pieces)
    ]
    for copy in [*first, *copies]:
        copy.start()
    for copy in first:
        copy.wait()
    tall = step * parts * depth
    for i, copy in enumerate(copies):
        copy.wait()
        values = held_ref[i * step : (i + 1) * step].astype(jnp.float32).reshape(tall, width)
        wide_ref[i * tall : (i + 1) * tall, :] = values
        for c in range(parts):
            for x in range(depth):
                piece = wide_ref[pl.ds(i * tall + c * depth + x, step, stride=parts * depth), :]
                if signs_ref is not None:
                    piece = piece * (2 * signs_ref[x : x + 1, :] - 1).astype(jnp.float32)
                low = c * snaps + i * step
                out_ref[low : low + step, x * width : (x + 1) * width] = piece.astype(out_ref.dtype)


def field_kernel(flags_ref, field_ref, lanes_ref, flat_ref, rim_a_ref, rim_b_ref, held_ref, wide_ref, sems):
    snaps, _, depth, width = field_ref.shape
    to_lanes(field_ref, held_ref, sems, wide_ref, lanes_ref)
    flat_ref[...] = lanes_ref[: 2 * snaps, :]
    odd = flags_ref[1] == 1
    first = lanes_ref[snaps:, :width].astype(jnp.float32)
    last = lanes_ref[snaps:, (depth - 1) * width :].astype(jnp.float32)
    rim_a_ref[...] = jnp.where(odd, first, last).astype(rim_a_ref.dtype)
    rim_b_ref[...] = jnp.where(odd, last, first).astype(rim_b_ref.dtype)


def velocity_kernel(
    flags_ref,
    velocity_ref,
    test_ref,
    signs_ref,
    pair_ref,
    matrix_ref,
    held_ref,
    wide_ref,
    sems,
    bits_ref,
    bits_sem,
    held_signs_ref,
    signs_sem,
):
    snaps, parts = velocity_ref.shape[:2]
    copy_signs = pltpu.make_async_copy(signs_ref, held_signs_ref, signs_sem)
    copy = pltpu.make_async_copy(test_ref, bits_ref, bits_sem)
    copy.start()
    to_lanes(velocity_ref, held_ref, sems, wide_ref, pair_ref, held_signs_ref, [copy_signs])
    copy.wait()
    columns = bits_ref.shape[0]
    width = wide_ref.shape[1]
    for low in range(0, bits_ref.shape[1], width):
        wide_ref[:columns, :] = (2 * bits_ref[:, low : low + width] - 1).astype(jnp.float32)
        for c in range(2 * parts):
            piece = wide_ref[pl.ds(c, snaps, stride=2 * parts), :]
            matrix_ref[c * snaps : (c + 1) * snaps, low : low + width] = piece.astype(matrix_ref.dtype)


def relay(kernel, flags, inputs, in_vmem, shapes, scratch=()):
    snaps, parts, depth, width = inputs[0].shape
    held = [pltpu.VMEM(inputs[0].shape, inputs[0].dtype), pltpu.VMEM((snaps * parts * depth, width), jnp.float32)]
    return pl.pallas_call(
        kernel,
        out_shape=[jax.ShapeDtypeStruct(shape, dtype) for shape, dtype in shapes],
        in_specs=[SMEM] + [pl.BlockSpec(memory_space=pl.ANY)] * len(inputs) + [VMEM] * len(in_vmem),
        out_specs=[VMEM] * len(shapes),
        scratch_shapes=held + [pltpu.SemaphoreType.DMA((4,))] + list(scratch),
        compiler_params=pltpu.CompilerParams(vmem_limit_bytes=8 << 20),
        name=kernel.__name__,
    )(flags, *[pltpu.with_memory_space_constraint(array, pltpu.HBM) for array in inputs], *in_vmem)


def curl_kernel(flags_ref, field_ref, plane_a_ref, plane_b_ref, rim_a_ref, rim_b_ref, signs_ref, current_ref):
    snaps = rim_a_ref.shape[0] // 2
    width = rim_a_ref.shape[1]
    depth = field_ref.shape[1] // width
    upward = 0.5 - flags_ref[0].astype(jnp.float32)
    odd_block = flags_ref[1] == 1
    lane = lax.broadcasted_iota(jnp.int32, (snaps, width), 1)

    def field(c, x):
        return lanes_of(field_ref.at[c * snaps : (c + 1) * snaps], x, width).astype(jnp.float32)

    def over_x(c, x):
        rim_a = rim_a_ref[(c - 1) * snaps : c * snaps, :].astype(jnp.float32)
        rim_b = rim_b_ref[(c - 1) * snaps : c * snaps, :].astype(jnp.float32)
        low = field(c, x - 1) if x else jnp.where(odd_block, rim_a, rim_b)
        high = field(c, x + 1) if x < depth - 1 else jnp.where(odd_block, rim_b, rim_a)
        return (high - low) * 0.5

    def over_y(c, x):
        values = field(c, x)
        low = jnp.where(lane == 0, 0.0, pltpu.roll(values, 1, 1))
        high = jnp.where(lane == width - 1, 0.0, pltpu.roll(values, width - 1, 1))
        return (high - low) * 0.5

    def over_z(c, x):
        a = lanes_of(plane_a_ref.at[c * snaps : (c + 1) * snaps], x, width).astype(jnp.float32)
        b = lanes_of(plane_b_ref.at[c * snaps : (c + 1) * snaps], x, width).astype(jnp.float32)
        return (a - b) * upward

    for x in range(depth):
        sign = (2 * signs_ref[x : x + 1, :] - 1).astype(jnp.float32)
        current = (
            over_y(2, x) - over_z(1, x),
            over_z(0, x) - over_x(2, x),
            over_x(1, x) - over_y(0, x),
        )
        for c, values in enumerate(current):
            current_ref[c * snaps : (c + 1) * snaps, x * width : (x + 1) * width] = (values * sign).astype(
                current_ref.dtype
            )


def parts_kernel(flags_ref, wanted_ref, pair_ref, other_ref, current_ref, other_current_ref, matrix_ref, *refs):
    part_refs, held_ref = refs[:-1], refs[-1]
    rows, points = current_ref.shape
    width = held_ref.shape[1]
    halves = matrix_ref.shape[1] // width
    own_sign = (1 - 2 * flags_ref[0]).astype(jnp.float32)

    def sketch(values_ref, matrix):
        return lax.dot_general(values_ref, matrix, (TN, ((), ())), preferred_element_type=jnp.float32)

    plain = matrix_ref[...]
    turned = (plain.astype(jnp.float32) * own_sign).astype(plain.dtype)
    total = sketch(pair_ref[-rows:, :], turned[:rows]) + sketch(other_ref[-rows:, :], plain[:rows])
    total = total + sketch(current_ref[...], turned[rows:]) + sketch(other_current_ref[...], plain[rows:])
    for half in range(halves):
        held_ref[pl.ds(half, points, stride=halves), :] = total[:, half * width : (half + 1) * width]
    samples = part_refs[0].shape[0] // halves
    batch = 16
    for slot, part_ref in enumerate(part_refs):
        for first in range(0, samples, batch):
            at = [pl.multiple_of(wanted_ref[slot * samples + first + i], halves) for i in range(batch)]
            values = [held_ref[pl.ds(start, halves), :] for start in at]
            for i in range(batch):
                part_ref[(first + i) * halves : (first + i + 1) * halves, :] = values[i]


def gram_kernel(signs_ref, *refs):
    parts, (picked_ref, packed_ref, held_ref) = refs[:-3], refs[-3:]
    total = signs_ref[0] * parts[0][...]
    for slot in range(1, len(parts)):
        total = total + signs_ref[slot] * parts[slot][...]
    held_ref[...] = total
    samples, wide = picked_ref.shape
    width = held_ref.shape[1]
    halves = wide // width
    picked = [held_ref[pl.ds(half, samples, stride=halves), :] for half in range(halves)]
    picked = jnp.concatenate(picked, axis=1)
    picked_ref[...] = picked
    pack(product(picked.T, picked, NN) * signs_ref[len(parts)], packed_ref)


def product(a, b, dims):
    return lax.dot_general(
        a, b, (dims, ((), ())), precision=lax.Precision.HIGHEST, preferred_element_type=jnp.float32
    )


def in_three(x):
    high = x.astype(jnp.bfloat16)
    left = x - high.astype(jnp.float32)
    middle = left.astype(jnp.bfloat16)
    return high, middle, (left - middle.astype(jnp.float32)).astype(jnp.bfloat16)


def outer(a, b):
    (a0, a1, a2), (b0, b1, b2) = in_three(a), in_three(b)
    left = jnp.concatenate([a0, a0, a1, a0, a2, a1])
    right = jnp.concatenate([b0, b1, b0, b2, b0, b1])
    return lax.dot_general(left, right, (TN, ((), ())), preferred_element_type=jnp.float32)


def eliminate(a_ref, z_ref):
    n = a_ref.shape[0]
    blocks = n // ROWS
    row = lax.broadcasted_iota(jnp.int32, (ROWS, n), 0)
    lane = lax.broadcasted_iota(jnp.int32, (ROWS, n), 1)

    def spread(x):
        return jnp.broadcast_to(x, (ROWS, n))

    def column(block, c):
        return spread(block[:, c : c + 1])

    def line(block, k):
        return spread(block[k : k + 1, :])

    rest = [a_ref[b * ROWS : (b + 1) * ROWS, :] for b in range(blocks)]
    rest_z = [jnp.where(lane == row + b * ROWS, 1.0, 0.0) for b in range(blocks)]
    columns = [column(rest[0], c) for c in range(ROWS)]
    for b in range(blocks):
        start = b * ROWS
        pivots = {(k, c): line(columns[c], k) for c in range(ROWS) for k in range(c + 1)}
        top = [line(rest[b], k) for k in range(ROWS)]
        top_z = [line(rest_z[b], k) for k in range(ROWS)]
        following = range(b + 1, min(b + 2, blocks))
        for g in following:
            next_old = [column(rest[g], start + c) for c in range(ROWS)]
            columns = [column(rest[g], start + ROWS + c) for c in range(ROWS)]
        inverse = []
        for k in range(ROWS):
            inverse.append(1.0 / pivots[k, k])
            for i in range(k + 1, ROWS):
                times = pivots[k, i] * inverse[k]
                for c in range(i, ROWS):
                    pivots[i, c] = pivots[i, c] - times * pivots[k, c]
                top[i] = top[i] - times * top[k]
                top_z[i] = top_z[i] - times * top_z[k]
            for g in following:
                times = next_old[k] * inverse[k]
                columns = [values - times * line(next_old[k], c) for c, values in enumerate(columns)]
                for c in range(k + 1, ROWS):
                    next_old[c] = next_old[c] - times * pivots[k, c]
                rest[g] = rest[g] - times * top[k]
                rest_z[g] = rest_z[g] - times * top_z[k]
        for g in range(b + 2, min(b + NEAR, blocks)):
            old = [column(rest[g], start + c) for c in range(ROWS)]
            for k in range(ROWS):
                times = old[k] * inverse[k]
                for c in range(k + 1, ROWS):
                    old[c] = old[c] - times * pivots[k, c]
                rest[g] = rest[g] - times * top[k]
                rest_z[g] = rest_z[g] - times * top_z[k]
        done, done_z = jnp.zeros((ROWS, n), jnp.float32), jnp.zeros((ROWS, n), jnp.float32)
        for k in range(ROWS):
            scale = lax.rsqrt(pivots[k, k])
            done = jnp.where(row == k, top[k] * scale, done)
            done_z = jnp.where(row == k, top_z[k] * scale, done_z)
        done = jnp.where(lane >= row + start, done, 0.0)
        a_ref[start : start + ROWS, :] = done
        z_ref[start : start + ROWS, :] = done_z
        far = (b + NEAR) * ROWS
        if far < n:
            update = outer(done[:, far:], jnp.concatenate([done, done_z], axis=1))
            for g in range(b + NEAR, blocks):
                low = g * ROWS - far
                rest[g] = rest[g] - update[low : low + ROWS, :n]
                rest_z[g] = rest_z[g] - update[low : low + ROWS, n:]


def pack(gram, packed_ref):
    n = gram.shape[0]
    q, h = n // 4, n // 2
    lane = lax.broadcasted_iota(jnp.int32, (q, h), 1)
    packed_ref[:q, :] = gram[:q, :]
    packed_ref[q:h, :h] = jnp.where(lane < q, gram[h : h + q, h:], gram[q:h, :h])
    packed_ref[q:h, h:] = gram[q:h, h:]
    packed_ref[h:, :h] = gram[h + q : h + q + q // 2, h:]
    packed_ref[h:, h:] = gram[h + q + q // 2 :, h:]


def unpack(packed):
    n = packed.shape[1]
    q, h = n // 4, n // 2
    row = lax.broadcasted_iota(jnp.int32, (h, h), 0)
    lane = lax.broadcasted_iota(jnp.int32, (h, h), 1)
    top = packed[:h, :h]
    first = jnp.where((row >= q) & (lane < q), top.T, top)
    bottom = jnp.concatenate([packed[q:h, :h], packed[h:, :h], packed[h:, h:]])
    last = jnp.where((row < q) & (lane >= q), bottom.T, bottom)
    return first, packed[:h, h:], last


def parity_sign(a, b):
    both = jnp.bitwise_and(a, b)
    return 1.0 - 2.0 * (lax.population_count(both) % 2).astype(jnp.float32)


def doubled(rows, bit):
    return jnp.concatenate([rows, lax.ppermute(rows, "mix", xor_route(lax.axis_size("mix"), bit))])


def sampled_mixing(flags, pair, other, current, matrix, wanted):
    planes = lax.axis_size("mix")
    mine = lax.axis_index("mix")
    targets, samples = wanted.shape
    halves = matrix.shape[1] // LANES
    part = ((samples * halves, LANES), jnp.float32)
    other_current = lax.ppermute(current, "mix", xor_route(planes, 1))
    inputs = (flags, wanted.reshape(-1) * halves, pair, other, current, other_current, matrix)
    scratch = ((current.shape[1] * halves, LANES),)
    parts = local(parts_kernel, inputs, [part] * targets, scratch, megabytes=12, scalars=2)
    hops = [0]
    for level in range(planes.bit_length() - 2, 0, -1):
        hops += [hop ^ 1 << level for hop in hops]
    arrived = [parts[0]] + [lax.ppermute(part, "mix", xor_route(planes, k)) for part, k in zip(parts[1:], hops[1:])]
    return arrived, [parity_sign(mine, (mine ^ k) - mine % 2) for k in hops]


def whole_mixing(pair, current, matrix, wanted):
    planes = lax.axis_size("mix")
    mine = lax.axis_index("mix")
    snapshot = jnp.concatenate([pair[-current.shape[0] :], current])
    values = lax.dot_general(snapshot, matrix, (((0,), (0,)), ((), ())), preferred_element_type=jnp.float32)
    for level in range(planes.bit_length() - 1):
        partner = lax.ppermute(values, "mix", xor_route(planes, 1 << level))
        upper_bit = mine // (1 << level) % 2
        values = jnp.where(upper_bit == 1, partner - values, values + partner)
    return [jnp.take(values, wanted[0], axis=0).reshape(-1, LANES)], [jnp.float32(1.0)]


def sum_over_mesh(packed):
    planes, blocks = lax.axis_size("mix"), lax.axis_size("row")
    half_rows = packed.shape[0] // 2
    low, high = packed[:half_rows], packed[half_rows:]
    if planes > 8 or blocks != 4:
        low, high = lax.psum((low, high), MESH_AXES)
        return low, high, jnp.int32(0)
    core = lax.axis_index("mix") % 2
    half = jnp.where(core == 0, low, high)
    half = half + lax.ppermute(jnp.where(core == 0, high, low), "mix", xor_route(planes, 1))
    half = half + sum(lax.ppermute(half, "mix", xor_route(planes, k)) for k in range(2, planes, 2))
    half = half + sum(lax.ppermute(half, "row", xor_route(blocks, k)) for k in range(blocks - 1, 0, -1))
    return half, lax.ppermute(half, "mix", xor_route(planes, 1)), core


def finish_kernel(core_ref, half_ref, other_ref, picked_ref, basis_ref, factor_ref, a_ref, first_ref, second_ref):
    side = a_ref.shape[0]
    half, other = half_ref[...], other_ref[...]
    swap = core_ref[0] != 0
    packed = jnp.concatenate([jnp.where(swap, other, half), jnp.where(swap, half, other)])
    corner, right, last = unpack(packed)
    a_ref[...] = corner
    eliminate(a_ref, first_ref)
    first = first_ref[...]
    across = product(first, right, NN)
    down = product(right.T, first, NT)
    factor_ref[:side, :side] = a_ref[...]
    factor_ref[:side, side:] = across
    factor_ref[side:, :side] = jnp.zeros_like(across)
    a_ref[...] = last - product(down, across, NN)
    solved = product(picked_ref[:, :side], first, NT)
    basis_ref[:, :side] = solved
    left_over = picked_ref[:, side:] - product(solved, across, NN)
    eliminate(a_ref, second_ref)
    basis_ref[:, side:] = product(left_over, second_ref[...], NT)
    factor_ref[side:, side:] = a_ref[...]


def finish(half, other, core, picked):
    n = picked.shape[1]
    shapes = [(picked.shape, jnp.float32), ((n, n), jnp.float32)]
    scratch = ((n // 2, n // 2),) * 3
    return local(finish_kernel, (core.reshape(1), half, other, picked), shapes, scratch)


def on_device(velocity, field_b, test_signs, row_signs, sample_index):
    snaps, parts, _, depth, width = field_b.shape
    sketch_width = test_signs.shape[1]
    planes, blocks = lax.axis_size("mix"), lax.axis_size("row")
    samples = sample_index.shape[-1]
    points = depth * width
    flags = jnp.stack([lax.axis_index("mix") % 2, lax.axis_index("row") % 2]).astype(jnp.int32)
    signs = row_signs[0]
    lanes = ((parts * snaps, points), jnp.bfloat16)
    flat = ((2 * snaps, points), jnp.bfloat16)
    rim = ((2 * snaps, width), jnp.bfloat16)
    sampled_bytes = (planes // 2 - 1) * samples * sketch_width
    whole_bytes = (planes.bit_length() - 1) * points * sketch_width
    sampled = sampled_bytes < whole_bytes
    wanted = sample_index.reshape(1, -1)
    if sampled:
        wanted = doubled(wanted, planes // 2)
    field, flat, rim_a, rim_b = relay(field_kernel, flags, [field_b[:, :, 0]], [], [lanes, flat, rim, rim])
    plane_b = lax.ppermute(flat, "mix", pair_route(planes, 1))
    rim_a = lax.ppermute(rim_a, "row", pair_route(blocks, 0))
    rim_b = lax.ppermute(rim_b, "row", pair_route(blocks, 1))
    matrix = ((2 * parts * snaps, sketch_width), jnp.bfloat16)
    scratch = [pltpu.VMEM(test_signs.shape, jnp.int32), pltpu.SemaphoreType.DMA]
    scratch += [pltpu.VMEM(signs.shape, jnp.int32), pltpu.SemaphoreType.DMA]
    inputs = [velocity[:, :, 0], test_signs, signs]
    pair, matrix = relay(velocity_kernel, flags, inputs, [], [lanes, matrix], scratch)
    plane_a = lax.ppermute(flat, "mix", pair_route(planes, 0))
    pair, wanted = lax.optimization_barrier((pair, wanted))
    other = lax.ppermute(pair, "mix", pair_route(planes, 0))
    if sampled:
        for level in range(planes.bit_length() - 3, 0, -1):
            wanted = doubled(wanted, 1 << level)
    (current,) = local(curl_kernel, (flags, field, plane_a, plane_b, rim_a, rim_b, signs), [lanes])
    if sampled:
        added, part_signs = sampled_mixing(flags, pair, other, current, matrix, wanted)
    else:
        added, part_signs = whole_mixing(pair, current, matrix, wanted)
    scale = 1.0 / math.sqrt(6 * snaps * planes)
    factors = jnp.stack([sign * scale for sign in part_signs] + [jnp.float32(1.0 / (planes * blocks * samples))])
    picked, packed = local(
        gram_kernel,
        (factors, *added),
        [((samples, sketch_width), jnp.float32), ((sketch_width * 5 // 8, sketch_width), jnp.float32)],
        (added[0].shape,),
    )
    basis_rows, factor = finish(*sum_over_mesh(packed), picked)
    return basis_rows.reshape(sample_index.shape + (sketch_width,)), factor


def solution(mesh):
    return jax.shard_map(
        on_device,
        mesh=mesh,
        in_specs=(
            P(None, None, "mix", "row", None),
            P(None, None, "mix", "row", None),
            P(),
            P("mix", "row", None),
            P("mix", "row", None),
        ),
        out_specs=(P("mix", "row", None, None), P()),
        check_vma=False,
    )
```
